32 devices in a mesh: band: 4 (over y, core), ma: 8 (over z, x).
Axes of the slice: x: 2, y: 2, z: 4, core: 2. Of those that a mesh axis runs over, the one named last changes fastest.
Arguments:
- sky_maps: bfloat16 [64, 64, 2, 16384], P(None, ('band', 'ma')), may hold values from -6 to 6
- hi_cycles: int32 [64], P(('band', 'ma')), may hold values from 4096 to 8191, as said below
- lo_cycles: int32 [64], P(('band', 'ma')), may hold values from 1024 to 2047, as said below
- azimuth_orders: int32 [128], replicated, may hold values from 0 to 3071, as said below
- legendre_hi: bfloat16 [128, 3072, 64], P(('band', 'ma')), may hold values from -0.75 to 0.75
- legendre_lo: bfloat16 [128, 3072, 64], P(('band', 'ma')), may hold values from -0.109375 to 0.109375
- beam_weights: float32 [3072], replicated, may hold values from 0.05 to 1
Outputs:
- smoothed_maps: float32 [64, 64, 2, 4096], P(None, ('band', 'ma'))
The draws below stay inside these ranges and needn't reach their ends.
Inputs may be any that keep to these rules, and one draw needn't show every extreme that they name: `hi_cycles`: distinct northern equatorial-belt cycles. `lo_cycles`: distinct northern equatorial-belt cycles. `azimuth_orders`: distinct orders.
All inputs are finite; a program needn't handle non-finite values.
Results may differ from the reference program's by a relative error of at most 0.0038.
Values may be sent and summed in bfloat16 or wider, within the bound.
No kernel may reach another device: no remote copies, remote signals or barrier semaphores. Data moves between devices by JAX's collectives and lax.ppermute only.
A program may use at most 192 MiB of HBM per device.

```python
import math
import jax
import jax.numpy as jnp
from jax import lax

NSIDE_HI = 4096
NSIDE_LO = 1024
LROWS = 3072
NMAPS = 64
NPIX_HI = 16384
NPIX_LO = 4096
NPAIRS = 64
NLPAIRS = 64
MSEL = 128


def pick_distinct(base_key, how_many, span_size):
    middle = jax.random.permutation(base_key, span_size - 2)[:how_many - 2] + 1
    ends = jnp.array([0, span_size - 1], dtype=jnp.int32)
    chosen = jnp.concatenate([ends, middle.astype(jnp.int32)])
    shuffle = jax.random.permutation(jax.random.fold_in(base_key, 11), how_many)
    return chosen[shuffle]


def draw_hi_cycles(key, part):
    return NSIDE_HI + pick_distinct(jax.random.fold_in(key, 1), NPAIRS, NSIDE_HI)


def draw_lo_cycles(key, part):
    return NSIDE_LO + pick_distinct(jax.random.fold_in(key, 2), NLPAIRS, NSIDE_LO)


def draw_azimuth_orders(key, part):
    return pick_distinct(jax.random.fold_in(key, 3), MSEL, LROWS)


def levels(rng, dims, split, least, top_value):
    def one(dim, parts):
        heights = jax.random.uniform(jax.random.fold_in(jax.random.fold_in(rng, 6), dim), (parts,), jnp.float32, least / len(split), top_value / len(split))
        return jnp.repeat(jnp.exp(heights), dims[dim] // parts).reshape((-1,) + (1,) * (len(dims) - dim - 1))

    gain = one(*split[0])
    for cut in split[1:]:
        gain = gain * one(*cut)
    return gain


def noise(stream_key, shape, width, bound, pieces=(), held_as=jnp.bfloat16):
    level = levels(stream_key, shape, pieces, -0.22, 0.18) if pieces else 1.0
    result = jax.random.normal(stream_key, shape, jnp.float32) * width * level
    return jnp.minimum(jnp.maximum(result, -bound), bound).astype(held_as)


def setup_inputs(seed: int = 0) -> dict:
    key_of = jax.random.split(jax.random.key(seed), 8)
    return {
        "sky_maps": noise(key_of[0], (NMAPS, NPAIRS, 2, NPIX_HI), 1.0, 6.0, ((1, 32),)),
        "hi_cycles": draw_hi_cycles(jax.random.fold_in(key_of[7], 71), 0),
        "lo_cycles": draw_lo_cycles(jax.random.fold_in(key_of[7], 71), 0),
        "azimuth_orders": draw_azimuth_orders(jax.random.fold_in(key_of[7], 71), 0),
        "legendre_hi": noise(key_of[4], (MSEL, LROWS, NPAIRS), NPAIRS ** -0.5, 0.75, ((0, 32),)),
        "legendre_lo": noise(key_of[5], (MSEL, LROWS, NLPAIRS), LROWS ** -0.5, 0.109375, ((0, 32),)),
        "beam_weights": jnp.clip(jnp.exp(jax.random.uniform(key_of[6], (LROWS,), jnp.float32, math.log(0.05), math.log(1.0))), 0.05, 1.0),
    }


def angle_grid(first, second, length):
    product = first[:, None] * second[None, :] % length
    return product.astype(jnp.float32) * (2.0 * math.pi / length)

def cycle_offsets(cycle_ids, side_count):
    return ((cycle_ids - side_count + 1) % 2).astype(jnp.float32)

def reference(sky_maps, hi_cycles, lo_cycles, azimuth_orders, legendre_hi, legendre_lo, beam_weights):
    map_count = sky_maps.shape[0]
    pair_total = sky_maps.shape[1]
    select_total = azimuth_orders.shape[0]
    pixels_hi = jnp.arange(NPIX_HI, dtype=jnp.int32)
    angles = angle_grid(pixels_hi, azimuth_orders, NPIX_HI)
    forward_table = jnp.concatenate([jnp.cos(angles), jnp.sin(angles)], axis=1).astype(jnp.bfloat16)
    raw_sums = jnp.dot(sky_maps.reshape(-1, NPIX_HI), forward_table, preferred_element_type=jnp.float32)
    raw_sums = raw_sums.reshape(map_count, pair_total, 2, 2, select_total)
    real_raw = raw_sums[:, :, :, 0]
    imag_raw = -raw_sums[:, :, :, 1]
    offsets_hi = cycle_offsets(hi_cycles, NSIDE_HI)
    theta_hi = math.pi * offsets_hi[:, None] * azimuth_orders.astype(jnp.float32)[None, :] / NPIX_HI
    cos_hi = jnp.cos(theta_hi)[None, :, None, :]
    sin_hi = jnp.sin(theta_hi)[None, :, None, :]
    scale_hi = 1.0 / math.sqrt(NPIX_HI)
    real_coef = (real_raw * cos_hi + imag_raw * sin_hi) * scale_hi
    imag_coef = (imag_raw * cos_hi - real_raw * sin_hi) * scale_hi
    stacked = jnp.stack([real_coef, imag_coef], axis=3)
    coeffs = jnp.transpose(stacked, (4, 1, 2, 3, 0)).reshape(select_total, pair_total, 4 * map_count).astype(jnp.bfloat16)
    degrees = jnp.arange(LROWS, dtype=jnp.int32)
    half_cols = 2 * map_count

    def per_order(items):
        block_hi, block_lo, gathered, order = items
        parity = (degrees + order) % 2
        signs_lm = 1.0 - 2.0 * parity.astype(jnp.float32)
        beam_mask = jnp.where(degrees >= order, beam_weights, jnp.zeros_like(beam_weights))
        analysis = jnp.dot(block_hi, gathered, preferred_element_type=jnp.float32)
        harmonic = analysis[:, :half_cols] + signs_lm[:, None] * analysis[:, half_cols:]
        weighted = beam_mask[:, None] * harmonic
        paired = jnp.concatenate([weighted, signs_lm[:, None] * weighted], axis=1)
        return jnp.dot(block_lo.astype(jnp.float32).T, paired, precision=lax.Precision.HIGHEST, preferred_element_type=jnp.float32)
    synthesized = lax.map(per_order, (legendre_hi, legendre_lo, coeffs, azimuth_orders))
    low_total = synthesized.shape[1]
    parts_low = synthesized.reshape(select_total, low_total, 2, 2, map_count)
    real_low = parts_low[:, :, :, 0]
    imag_low = parts_low[:, :, :, 1]
    offsets_lo = cycle_offsets(lo_cycles, NSIDE_LO)
    theta_lo = math.pi * azimuth_orders.astype(jnp.float32)[:, None] * offsets_lo[None, :] / NPIX_LO
    cos_lo = jnp.cos(theta_lo)[:, :, None, None]
    sin_lo = jnp.sin(theta_lo)[:, :, None, None]
    real_rot = real_low * cos_lo - imag_low * sin_lo
    imag_rot = imag_low * cos_lo + real_low * sin_lo
    spectra = jnp.stack([real_rot, imag_rot], axis=0)
    spectra = jnp.transpose(spectra, (4, 2, 3, 0, 1)).reshape(-1, 2 * select_total)
    pixels_lo = jnp.arange(NPIX_LO, dtype=jnp.int32)
    angles_lo = angle_grid(azimuth_orders, pixels_lo, NPIX_LO)
    inverse_table = jnp.concatenate([jnp.cos(angles_lo), -jnp.sin(angles_lo)], axis=0)
    pixels_out = jnp.dot(spectra, inverse_table, precision=lax.Precision.HIGHEST, preferred_element_type=jnp.float32)
    pixels_out = pixels_out * math.sqrt(2.0 / select_total)
    return pixels_out.reshape(map_count, low_total, 2, NPIX_LO)
```

```python
import functools
import math

import jax
import jax.numpy as jnp
from jax import lax
from jax.experimental import pallas as pl
from jax.experimental.pallas import tpu as pltpu
from jax.sharding import PartitionSpec as P

NSIDE_HI = 4096
NSIDE_LO = 1024
NPIX_HI = 16384
NPIX_LO = 4096

LANES = 128
HEMIS = 2
BF16_ROWS = 16
F32_ROWS = 8
F32 = jnp.float32
BF16 = jnp.bfloat16


def unit_circle(steps, length):
    quarter = length // 4
    quadrant = (steps + quarter // 2) // quarter
    rest = steps - quadrant * quarter
    angle = rest.astype(F32) * (2.0 * math.pi / length)
    square = angle * angle
    sine = square * (1.0 / 362880.0) - 1.0 / 5040.0
    sine = square * sine + 1.0 / 120.0
    sine = square * sine - 1.0 / 6.0
    sine = angle + angle * (square * sine)
    cosine = square * (-1.0 / 3628800.0) + 1.0 / 40320.0
    cosine = square * cosine - 1.0 / 720.0
    cosine = square * cosine + 1.0 / 24.0
    cosine = square * cosine - 0.5
    cosine = 1.0 + square * cosine
    odd = (quadrant & 1) == 1
    big = jnp.where(odd, sine, cosine)
    small = jnp.where(odd, cosine, sine)
    cos_out = jnp.where(((quadrant + 1) & 2) == 2, -big, big)
    sin_out = jnp.where((quadrant & 2) == 2, -small, small)
    return cos_out, sin_out


def iota(shape, dim):
    return lax.broadcasted_iota(jnp.int32, shape, dim)


def split(value):
    high = value.astype(BF16)
    return high, (value - high.astype(F32)).astype(BF16)


def analyse_kernel(hi_ref, orders_ref, sky_ref, out_ref, sky, table, sums, sems):
    chunks, rows_mp, blocks = sky.shape[:3]
    pairs = hi_ref.shape[0]
    orders = orders_ref[...]
    count = orders.shape[1]
    maps_here = rows_mp // pairs
    inner = BF16_ROWS // HEMIS
    copies = [
        pltpu.make_async_copy(
            sky_ref.at[pl.ds(c * rows_mp, rows_mp)], sky.at[c], sems.at[c]
        )
        for c in range(chunks)
    ]
    for copy in copies:
        copy.start()

    cos_l, sin_l = unit_circle(orders * iota((LANES, count), 0) & (NPIX_HI - 1), NPIX_HI)
    stride = inner * LANES
    cos_a, sin_a = unit_circle(
        orders * (stride * iota((blocks, count), 0)) & (NPIX_HI - 1), NPIX_HI
    )
    for a in range(blocks):
        ca, sa = cos_a[a : a + 1], sin_a[a : a + 1]
        table[a * LANES : (a + 1) * LANES, :count] = (ca * cos_l - sa * sin_l).astype(BF16)
        table[a * LANES : (a + 1) * LANES, count:] = (sa * cos_l + ca * sin_l).astype(BF16)

    scale = 1.0 / math.sqrt(NPIX_HI)
    phases = []
    for p in range(pairs):
        offset = (hi_ref[p] - NSIDE_HI + 1) & 1
        step = 2 * LANES * (iota((BF16_ROWS, count), 0) // HEMIS) + offset
        phases.append(unit_circle(orders * step & (2 * NPIX_HI - 1), 2 * NPIX_HI))
    cos_p = jnp.stack([c * scale for c, _ in phases])[None]
    sin_p = jnp.stack([s * scale for _, s in phases])[None]

    def reduce_blocks(value):
        value = value[:, :, :F32_ROWS] + value[:, :, F32_ROWS:]
        value = value.reshape(rows_mp, F32_ROWS, count)
        value = value + pltpu.roll(value, 4, 1)
        return value + pltpu.roll(value, 2, 1)

    for c in range(chunks):
        copies[c].wait()
        rows = jnp.concatenate(
            [sky[c, :, a].reshape(rows_mp * BF16_ROWS, LANES) for a in range(blocks)], axis=1
        )
        raw = jnp.dot(rows, table[...], preferred_element_type=F32)
        raw = raw.reshape(maps_here, pairs, BF16_ROWS, 2 * count)
        raw_c, raw_s = raw[..., :count], raw[..., count:]
        real = reduce_blocks(raw_c * cos_p - raw_s * sin_p)
        imag = reduce_blocks(-(raw_c * sin_p + raw_s * cos_p))
        for i in range(maps_here):
            for p in range(pairs):
                for h in range(HEMIS):
                    at = pl.ds(c * maps_here + i, 1)
                    sums[p, h, 0, at, :] = real[i * pairs + p, h : h + 1]
                    sums[p, h, 1, at, :] = imag[i * pairs + p, h : h + 1]
    out_ref[...] = sums[...].astype(BF16)


def harmonic_kernel(own_ref, coeff_ref, hi_ref, lo_ref, beam_ref, out_ref):
    order = own_ref[pl.program_id(0)]
    degrees = iota(beam_ref.shape, 1)
    sign = (1 - 2 * ((degrees + order) & 1)).astype(F32)
    weight = jnp.where(degrees >= order, beam_ref[...], 0.0)
    half = coeff_ref.shape[2] // 2
    coeff = jnp.concatenate([coeff_ref[0, :, :half], coeff_ref[0, :, half:]], axis=0)

    def both(table):
        flipped = (table.astype(F32) * sign).astype(BF16)
        return jnp.concatenate([table, flipped], axis=0)

    alm = lax.dot_general(
        coeff, both(hi_ref[0]), (((0,), (0,)), ((), ())), preferred_element_type=F32
    )
    high, low = split(alm * weight)
    table = both(lo_ref[0])
    dims = (((1,), (1,)), ((), ()))
    total = lax.dot_general(table, high, dims, preferred_element_type=F32)
    total += lax.dot_general(table, low, dims, preferred_element_type=F32)
    out_ref[0] = total.astype(out_ref.dtype)


def synthesise_kernel(
    lo_ref, orders_ref, column_ref, coeff_ref, out_ref, table_hi, table_lo, spectra, phase
):
    maps_here, pairs, blocks = out_ref.shape[:3]
    count = orders_ref.shape[1]
    map_count = spectra.shape[3]

    @pl.when(pl.program_id(0) == 0)
    def _():
        column = column_ref[...]
        orders = orders_ref[...]
        for a in range(blocks):
            pixel = a * (F32_ROWS // HEMIS * LANES) + iota((count, LANES), 1)
            cosine, sine = unit_circle(column * pixel & (NPIX_LO - 1), NPIX_LO)
            lanes = slice(a * LANES, (a + 1) * LANES)
            table_hi[:count, lanes], table_lo[:count, lanes] = split(cosine)
            table_hi[count:, lanes], table_lo[count:, lanes] = split(-sine)
        scale = math.sqrt(2.0 / count)
        for p in range(pairs):
            offset = (lo_ref[p] - NSIDE_LO + 1) & 1
            step = 2 * LANES * (iota((F32_ROWS, count), 0) // HEMIS) + offset
            cosine, sine = unit_circle(orders * step & (2 * NPIX_LO - 1), 2 * NPIX_LO)
            phase[p, 0] = cosine * scale
            phase[p, 1] = sine * scale
            turned = coeff_ref[p].astype(F32).T
            spectra[p] = turned.reshape(HEMIS, 2, map_count, count)

    rows = pl.ds(pl.multiple_of(pl.program_id(0) * maps_here, maps_here), maps_here)
    south = (iota((1, F32_ROWS, count), 1) & 1) == 1
    parts = []
    for p in range(pairs):
        def spread(c):
            north_rows = spectra[p, 0, c, rows, :]
            south_rows = spectra[p, 1, c, rows, :]
            return jnp.where(south, south_rows[:, None, :], north_rows[:, None, :])

        real, imag = spread(0), spread(1)
        cosine, sine = phase[p, 0][None], phase[p, 1][None]
        turned = jnp.concatenate(
            [real * cosine - imag * sine, imag * cosine + real * sine], axis=2
        )
        parts.append(turned.reshape(maps_here * F32_ROWS, 2 * count))
    high, low = split(jnp.concatenate(parts, axis=0))
    pixels = jnp.dot(high, table_hi[...], preferred_element_type=F32)
    pixels += jnp.dot(low, table_hi[...], preferred_element_type=F32)
    pixels += jnp.dot(high, table_lo[...], preferred_element_type=F32)
    pixels = pixels.reshape(pairs, maps_here, F32_ROWS, blocks * LANES)
    for p in range(pairs):
        for a in range(blocks):
            out_ref[:, p, a] = pixels[p, :, :, a * LANES : (a + 1) * LANES]


def vmem():
    return pl.BlockSpec(memory_space=pltpu.VMEM)


def smem():
    return pl.BlockSpec(memory_space=pltpu.SMEM)


def per_device(
    sky_maps, hi_cycles, lo_cycles, azimuth_orders, legendre_hi, legendre_lo, beam_weights
):
    axes = ("band", "ma")
    map_count, pairs = sky_maps.shape[:2]
    count = azimuth_orders.shape[0]
    owned, degree_count, pair_total = legendre_hi.shape
    low_total = legendre_lo.shape[2]
    order_row = azimuth_orders.reshape(1, count)
    order_column = azimuth_orders.reshape(count, 1)
    cols = HEMIS * 2 * map_count

    inner = BF16_ROWS // HEMIS
    blocks = NPIX_HI // (inner * LANES)
    sky = sky_maps.reshape(map_count, pairs, HEMIS, blocks, inner, LANES)
    sky = sky.transpose(0, 1, 3, 4, 2, 5)
    sky = sky.reshape(map_count * pairs, blocks, BF16_ROWS, LANES)
    rows_mp = 8 * pairs
    chunks = map_count * pairs // rows_mp
    coeffs = pl.pallas_call(
        analyse_kernel,
        out_shape=jax.ShapeDtypeStruct((pairs, HEMIS, 2, map_count, count), BF16),
        in_specs=[smem(), vmem(), pl.BlockSpec(memory_space=pl.ANY)],
        out_specs=vmem(),
        scratch_shapes=[
            pltpu.VMEM((chunks, rows_mp, blocks, BF16_ROWS, LANES), BF16),
            pltpu.VMEM((blocks * LANES, 2 * count), BF16),
            pltpu.VMEM((pairs, HEMIS, 2, map_count, count), F32),
            pltpu.SemaphoreType.DMA((chunks,)),
        ],
        compiler_params=pltpu.CompilerParams(vmem_limit_bytes=32 * 2**20),
        name="analyse",
    )(hi_cycles, order_row, sky)
    outgoing = coeffs.reshape(pairs, cols, count).transpose(2, 0, 1)
    received = lax.all_to_all(outgoing, axes, split_axis=0, concat_axis=1, tiled=True)

    own = lax.dynamic_slice_in_dim(azimuth_orders, lax.axis_index(axes) * owned, owned)
    harmonic = pl.pallas_call(
        harmonic_kernel,
        grid=(owned,),
        out_shape=jax.ShapeDtypeStruct((owned, HEMIS * low_total, 2 * map_count), BF16),
        in_specs=[
            smem(),
            pl.BlockSpec((1, pair_total, cols), lambda g: (g, 0, 0)),
            pl.BlockSpec((1, pair_total, degree_count), lambda g: (g, 0, 0)),
            pl.BlockSpec((1, low_total, degree_count), lambda g: (g, 0, 0)),
            pl.BlockSpec((1, degree_count), lambda g: (0, 0)),
        ],
        out_specs=pl.BlockSpec((1, HEMIS * low_total, 2 * map_count), lambda g: (g, 0, 0)),
        compiler_params=pltpu.CompilerParams(vmem_limit_bytes=32 * 2**20),
        name="harmonic",
    )(
        own,
        received,
        legendre_hi.transpose(0, 2, 1),
        legendre_lo.transpose(0, 2, 1),
        beam_weights.reshape(1, degree_count),
    )
    synthesised = harmonic.reshape(owned, HEMIS, low_total, 2 * map_count)
    synthesised = synthesised.transpose(0, 2, 1, 3).reshape(owned, low_total, cols)
    returned = lax.all_to_all(synthesised, axes, split_axis=1, concat_axis=0, tiled=True)

    blocks_lo = NPIX_LO // (F32_ROWS // HEMIS * LANES)
    maps_here = 16
    pixels = pl.pallas_call(
        synthesise_kernel,
        grid=(map_count // maps_here,),
        out_shape=jax.ShapeDtypeStruct((map_count, pairs, blocks_lo, F32_ROWS, LANES), F32),
        in_specs=[
            smem(),
            pl.BlockSpec((1, count), lambda i: (0, 0)),
            pl.BlockSpec((count, 1), lambda i: (0, 0)),
            pl.BlockSpec((pairs, count, cols), lambda i: (0, 0, 0)),
        ],
        out_specs=pl.BlockSpec(
            (maps_here, pairs, blocks_lo, F32_ROWS, LANES), lambda i: (i, 0, 0, 0, 0)
        ),
        scratch_shapes=[
            pltpu.VMEM((2 * count, blocks_lo * LANES), BF16),
            pltpu.VMEM((2 * count, blocks_lo * LANES), BF16),
            pltpu.VMEM((pairs, HEMIS, 2, map_count, count), F32),
            pltpu.VMEM((pairs, 2, F32_ROWS, count), F32),
        ],
        compiler_params=pltpu.CompilerParams(vmem_limit_bytes=32 * 2**20),
        name="synthesise",
    )(lo_cycles, order_row, order_column, returned.transpose(1, 0, 2))
    pixels = pixels.reshape(map_count, pairs, blocks_lo, F32_ROWS // HEMIS, HEMIS, LANES)
    pixels = pixels.transpose(0, 1, 4, 2, 3, 5)
    return pixels.reshape(map_count, pairs, HEMIS, NPIX_LO)


def solution(mesh):
    spread = ("band", "ma")
    return jax.shard_map(
        per_device,
        mesh=mesh,
        in_specs=(
            P(None, spread, None, None),
            P(spread),
            P(spread),
            P(),
            P(spread, None, None),
            P(spread, None, None),
            P(),
        ),
        out_specs=P(None, spread, None, None),
        check_vma=False,
    )
```

```python
import functools
import math

import jax
import jax.numpy as jnp
from jax import lax
from jax.experimental import pallas as pl
from jax.experimental.pallas import tpu as pltpu
from jax.sharding import PartitionSpec as P

NSIDE_HI = 4096
NSIDE_LO = 1024
NPIX_HI = 16384
NPIX_LO = 4096

LANES = 128
HEMIS = 2
BF16_ROWS = 16
F32_ROWS = 8
F32 = jnp.float32
BF16 = jnp.bfloat16


def unit_circle(steps, length):
    quarter = length // 4
    quadrant = (steps + quarter // 2) // quarter
    rest = steps - quadrant * quarter
    angle = rest.astype(F32) * (2.0 * math.pi / length)
    square = angle * angle
    sine = square * (1.0 / 362880.0) - 1.0 / 5040.0
    sine = square * sine + 1.0 / 120.0
    sine = square * sine - 1.0 / 6.0
    sine = angle + angle * (square * sine)
    cosine = square * (-1.0 / 3628800.0) + 1.0 / 40320.0
    cosine = square * cosine - 1.0 / 720.0
    cosine = square * cosine + 1.0 / 24.0
    cosine = square * cosine - 0.5
    cosine = 1.0 + square * cosine
    odd = (quadrant & 1) == 1
    big = jnp.where(odd, sine, cosine)
    small = jnp.where(odd, cosine, sine)
    cos_out = jnp.where(((quadrant + 1) & 2) == 2, -big, big)
    sin_out = jnp.where((quadrant & 2) == 2, -small, small)
    return cos_out, sin_out


def iota(shape, dim):
    return lax.broadcasted_iota(jnp.int32, shape, dim)


def split(value):
    high = value.astype(BF16)
    return high, (value - high.astype(F32)).astype(BF16)


def one_hot(shape, match):
    return jnp.where(match(iota(shape, 0), iota(shape, 1)), 1.0, 0.0).astype(BF16)


def dot_tn(lhs, rhs):
    return lax.dot_general(lhs, rhs, (((0,), (0,)), ((), ())), preferred_element_type=F32)


def dot_nt(lhs, rhs):
    return lax.dot_general(lhs, rhs, (((1,), (1,)), ((), ())), preferred_element_type=F32)


def dot_nn(lhs, rhs):
    return jnp.dot(lhs, rhs, preferred_element_type=F32)


def pair_rows(pairs):
    side = LANES * pairs
    return one_hot((side, side), lambda i, j: i == j % LANES * pairs + j // LANES)


def analyse_kernel(
    spans, hi_hbm, orders_hbm, sky_hbm, out_ref, hi, orders_ref, sky, table, raw_a, raw_b, sums, sems
):
    raws = (raw_a, raw_b)
    blocks = sky.shape[1]
    pairs = hi.shape[0]
    count = orders_ref.shape[1]
    map_count = sky.shape[0] // pairs
    inner = BF16_ROWS // HEMIS
    small = [
        pltpu.make_async_copy(orders_hbm, orders_ref, sems.at[0]),
        pltpu.make_async_copy(hi_hbm, hi, sems.at[1]),
    ]
    copies = []
    for c, (start, size) in enumerate(spans):
        part = pl.ds(start * pairs, size * pairs)
        copies.append(pltpu.make_async_copy(sky_hbm.at[part], sky.at[part], sems.at[2 + c]))
    for copy in small + copies:
        copy.start()

    gather = pair_rows(pairs)
    for copy in small:
        copy.wait()
    orders = orders_ref[...]
    cos_l, sin_l = unit_circle(orders * iota((LANES, count), 0) & (NPIX_HI - 1), NPIX_HI)
    stride = inner * LANES
    cos_a, sin_a = unit_circle(
        orders * (stride * iota((blocks, count), 0)) & (NPIX_HI - 1), NPIX_HI
    )
    scale = 1.0 / math.sqrt(NPIX_HI)
    cos_p, sin_p = [], []
    for p in range(pairs):
        offset = (hi[p] - NSIDE_HI + 1) & 1
        step = 2 * LANES * (iota((BF16_ROWS, count), 0) // HEMIS) + offset
        cosine, sine = unit_circle(orders * step & (2 * NPIX_HI - 1), 2 * NPIX_HI)
        cos_p.append(cosine * scale)
        sin_p.append(sine * scale)
    copies[0].wait()
    for a in range(blocks):
        ca, sa = cos_a[a : a + 1], sin_a[a : a + 1]
        table[a * LANES : (a + 1) * LANES, :count] = (ca * cos_l - sa * sin_l).astype(BF16)
        table[a * LANES : (a + 1) * LANES, count:] = (sa * cos_l + ca * sin_l).astype(BF16)

    def contract(c):
        start, size = spans[c]
        part = slice(start * pairs, (start + size) * pairs)
        rows = jnp.concatenate(
            [sky[part, a].reshape(size * pairs * BF16_ROWS, LANES) for a in range(blocks)], axis=1
        )
        raws[c % 2][: size * pairs * BF16_ROWS] = dot_nn(rows, table[...])

    sub = iota((1, F32_ROWS, count), 1)

    def sum_blocks(value):
        value = value[:, :F32_ROWS] + value[:, F32_ROWS:]
        low, high = value[:4], value[4:]
        first = sub < 4
        value = jnp.where(first, low, high) + pltpu.roll(jnp.where(first, high, low), 4, 1)
        low, high = value[:2], value[2:]
        first = (sub & 2) == 0
        value = jnp.where(first, low + pltpu.roll(low, 6, 1), high + pltpu.roll(high, 2, 1))
        low, high = value[:1], value[1:]
        first = (sub & 1) == 0
        north = jnp.where(first, low, pltpu.roll(high, 1, 1))
        south = jnp.where(first, pltpu.roll(low, 7, 1), high)
        return north[0], south[0]

    def finish(c):
        start, size = spans[c]
        rows = 8 * pairs * BF16_ROWS
        for group in range(size // 8):
            raw = raws[c % 2][group * rows : (group + 1) * rows]
            raw = raw.reshape(8, pairs, BF16_ROWS, 2 * count)
            at = start + group * 8
            for p in range(pairs):
                raw_c, raw_s = raw[:, p, :, :count], raw[:, p, :, count:]
                cosine, sine = cos_p[p][None], sin_p[p][None]
                real = sum_blocks(raw_c * cosine - raw_s * sine)
                imag = sum_blocks(raw_c * sine + raw_s * cosine)
                for h in range(HEMIS):
                    sums[p, h, 0, at : at + 8] = real[h]
                    sums[p, h, 1, at : at + 8] = -imag[h]

    contract(0)
    for c in range(1, len(spans)):
        copies[c].wait()
        contract(c)
        finish(c - 1)
    finish(len(spans) - 1)
    cols = HEMIS * 2 * map_count
    for j in range(count // LANES):
        lanes = slice(j * LANES, (j + 1) * LANES)
        held = [sums[p, :, :, :, lanes].reshape(cols, LANES).astype(BF16) for p in range(pairs)]
        block = dot_nt(gather, jnp.concatenate(held, axis=1))
        out_ref[j * LANES * pairs : (j + 1) * LANES * pairs] = block.astype(BF16)


def prepare_kernel(
    pairs, low_pairs, own_ref, hi_ref, lo_ref, beam_ref,
    hi_out, lo_out, weight_out, gather_out, scatter_out,
):
    slot, owned = pl.program_id(0), pl.num_programs(0)
    order = own_ref[slot]
    degrees = iota(beam_ref.shape, 1)
    sign = (1 - 2 * ((degrees + order) & 1)).astype(F32)
    weight_out[0] = jnp.where(degrees >= order, beam_ref[...], 0.0)
    for source, target in ((hi_ref, hi_out), (lo_ref, lo_out)):
        half = source.shape[1]
        target[0, :half] = source[0]
        target[0, half:] = (source[0].astype(F32) * sign).astype(BF16)

    rows, depth = gather_out.shape
    column = iota((1, depth), 1)
    hemi, pair = column // (depth // HEMIS), column % (depth // HEMIS)
    home = (pair // pairs * owned + slot) * pairs + pair % pairs + hemi * (rows // HEMIS)
    gather_out[...] = jnp.where(iota((rows, depth), 0) == home, 1.0, 0.0).astype(BF16)

    @pl.when(slot == 0)
    def _():
        shape = scatter_out.shape
        column = iota((1, shape[1]), 1)
        total = lo_ref.shape[1]
        part, pair = column // total, column % total
        home = (pair // low_pairs * owned + part) * low_pairs + pair % low_pairs
        scatter_out[...] = jnp.where(iota(shape, 0) == home, 1.0, 0.0).astype(BF16)


def inverse_table_kernel(pairs, column_ref, table_ref, gather_ref):
    count = column_ref.shape[0]
    column = column_ref[...]
    step = F32_ROWS // HEMIS * LANES
    cosine, sine = unit_circle(column * iota((count, LANES), 1) & (NPIX_LO - 1), NPIX_LO)
    cos_step, sin_step = unit_circle(
        jnp.broadcast_to(column * step & (NPIX_LO - 1), (count, LANES)), NPIX_LO
    )
    for a in range(table_ref.shape[1] // LANES):
        lanes = slice(a * LANES, (a + 1) * LANES)
        table_ref[:count, lanes] = cosine.astype(BF16)
        table_ref[count:, lanes] = (-sine).astype(BF16)
        cosine, sine = (
            cosine * cos_step - sine * sin_step,
            sine * cos_step + cosine * sin_step,
        )
    gather_ref[...] = pair_rows(pairs)


def harmonic_kernel(
    received_ref, gather_ref, scatter_ref, hi_ref, lo_ref, weight_ref, out_ref, held
):
    owned, depth = hi_ref.shape[:2]
    half = received_ref.shape[1] // HEMIS
    low_total = lo_ref.shape[1] // HEMIS
    received = jnp.concatenate([received_ref[:, :half], received_ref[:, half:]], axis=0)
    coeffs = dot_tn(received, gather_ref[...]).astype(BF16)
    for g in range(owned):
        alm = dot_nn(coeffs[:, g * depth : (g + 1) * depth], hi_ref[g]) * weight_ref[g]
        both = dot_nt(lo_ref[g], jnp.concatenate(split(alm), axis=0))
        total = (both[:, :half] + both[:, half:]).astype(BF16)
        for h in range(HEMIS):
            held[g * low_total : (g + 1) * low_total, h * half : (h + 1) * half] = total[
                h * low_total : (h + 1) * low_total
            ]
    out_ref[...] = dot_nn(scatter_ref[...], held[...]).astype(BF16)


def synthesise_kernel(
    lo_ref, orders_ref, table_ref, gather_ref, returned_ref, out_hbm,
    spectra, high, low, buf_a, buf_b, buf_c, buf_d, sems,
):
    buffers = (buf_a, buf_b, buf_c, buf_d)
    map_count, pairs, wide = buf_a.shape[:3]
    count = orders_ref.shape[1]
    orders = orders_ref[...]
    for j in range(count // LANES):
        rows = slice(j * LANES * pairs, (j + 1) * LANES * pairs)
        turned = dot_tn(returned_ref[rows], gather_ref[...])
        for p in range(pairs):
            spectra[p, :, j * LANES : (j + 1) * LANES] = turned[:, p * LANES : (p + 1) * LANES]

    scale = math.sqrt(2.0 / count)
    south = (iota((F32_ROWS, count), 0) & 1) == 1
    for p in range(pairs):
        offset = (lo_ref[p] - NSIDE_LO + 1) & 1
        step = 2 * LANES * (iota((F32_ROWS, count), 0) // HEMIS) + offset
        cosine, sine = unit_circle(orders * step & (2 * NPIX_LO - 1), 2 * NPIX_LO)
        cosine, sine = cosine * scale, sine * scale

        def turn(i):
            def spread(c):
                north = spectra[p, c * map_count + i : c * map_count + i + 1]
                at = (2 + c) * map_count + i
                return jnp.where(south, spectra[p, at : at + 1], north)

            real, imag = spread(0), spread(1)
            return real * cosine - imag * sine, imag * cosine + real * sine

        for i in range(0, map_count, 2):
            at = slice((p * map_count + i) * F32_ROWS, (p * map_count + i + 2) * F32_ROWS)
            for c, parts in enumerate(zip(turn(i), turn(i + 1))):
                lanes = slice(c * count, (c + 1) * count)
                high[at, lanes], low[at, lanes] = split(jnp.concatenate(parts, axis=0))

    copies = []
    for n, buffer in enumerate(buffers):
        table = table_ref[:, n * wide * LANES : (n + 1) * wide * LANES]
        pixels = dot_nn(high[...], table) + dot_nn(low[...], table)
        pixels = pixels.reshape(pairs, map_count, F32_ROWS, wide * LANES)
        for p in range(pairs):
            for a in range(wide):
                buffer[:, p, a] = pixels[p, :, :, a * LANES : (a + 1) * LANES]
        target = out_hbm.at[:, :, pl.ds(n * wide, wide)]
        copies.append(pltpu.make_async_copy(buffer, target, sems.at[n]))
        copies[-1].start()
    for copy in copies:
        copy.wait()


def vmem():
    return pl.BlockSpec(memory_space=pltpu.VMEM)


def smem():
    return pl.BlockSpec(memory_space=pltpu.SMEM)


def hbm():
    return pl.BlockSpec(memory_space=pltpu.HBM)


def params(mebibytes):
    return pltpu.CompilerParams(vmem_limit_bytes=mebibytes * 2**20)


def struct(shape, dtype):
    return jax.ShapeDtypeStruct(shape, dtype)


def per_device(
    sky_maps, hi_cycles, lo_cycles, azimuth_orders, legendre_hi, legendre_lo, beam_weights
):
    axes = ("band", "ma")
    map_count, pairs = sky_maps.shape[:2]
    low_pairs = lo_cycles.shape[0]
    count = azimuth_orders.shape[0]
    owned, degree_count, pair_total = legendre_hi.shape
    low_total = legendre_lo.shape[2]
    devices = count // owned
    order_row = azimuth_orders.reshape(1, count)
    order_column = azimuth_orders.reshape(count, 1)
    cols = HEMIS * 2 * map_count

    inner = BF16_ROWS // HEMIS
    blocks = NPIX_HI // (inner * LANES)
    sky = sky_maps.reshape(map_count, pairs, HEMIS, blocks, inner, LANES)
    sky = sky.transpose(0, 1, 3, 4, 2, 5)
    sky = sky.reshape(map_count * pairs, blocks, BF16_ROWS, LANES)
    quarter = map_count // 4
    spans = [(k * quarter, quarter) for k in range(3)]
    spans += [(3 * quarter, quarter // 2), (3 * quarter + quarter // 2, quarter // 2)]
    raw = pltpu.VMEM((quarter * pairs * BF16_ROWS, 2 * count), F32)
    outgoing = pl.pallas_call(
        functools.partial(analyse_kernel, spans),
        out_shape=struct((count * pairs, cols), BF16),
        in_specs=[hbm(), hbm(), hbm()],
        out_specs=vmem(),
        scratch_shapes=[
            pltpu.SMEM((pairs,), jnp.int32),
            pltpu.VMEM((1, count), jnp.int32),
            pltpu.VMEM((map_count * pairs, blocks, BF16_ROWS, LANES), BF16),
            pltpu.VMEM((blocks * LANES, 2 * count), BF16),
            raw,
            raw,
            pltpu.VMEM((pairs, HEMIS, 2, map_count, count), F32),
            pltpu.SemaphoreType.DMA((2 + len(spans),)),
        ],
        compiler_params=params(40),
        name="analyse",
    )(hi_cycles, order_row, sky)
    received = lax.all_to_all(
        outgoing.reshape(devices, owned * pairs, cols), axes, split_axis=0, concat_axis=0, tiled=True
    )

    own = lax.dynamic_slice_in_dim(azimuth_orders, lax.axis_index(axes) * owned, owned)
    rows, low_rows = count * pairs, count * low_pairs
    depth, low_depth = HEMIS * pair_total, HEMIS * low_total
    work = owned * degree_count * (depth + low_depth)
    hi_table, lo_table, weights, gather, scatter = pl.pallas_call(
        functools.partial(prepare_kernel, pairs, low_pairs),
        grid=(owned,),
        out_shape=[
            struct((owned, depth, degree_count), BF16),
            struct((owned, low_depth, degree_count), BF16),
            struct((owned, 1, degree_count), F32),
            struct((HEMIS * rows, owned * depth), BF16),
            struct((low_rows, owned * low_total), BF16),
        ],
        in_specs=[
            smem(),
            pl.BlockSpec((1, pair_total, degree_count), lambda g: (g, 0, 0)),
            pl.BlockSpec((1, low_total, degree_count), lambda g: (g, 0, 0)),
            pl.BlockSpec((1, degree_count), lambda g: (0, 0)),
        ],
        out_specs=[
            pl.BlockSpec((1, depth, degree_count), lambda g: (g, 0, 0)),
            pl.BlockSpec((1, low_depth, degree_count), lambda g: (g, 0, 0)),
            pl.BlockSpec((1, 1, degree_count), lambda g: (g, 0, 0)),
            pl.BlockSpec((HEMIS * rows, depth), lambda g: (0, g)),
            pl.BlockSpec((low_rows, owned * low_total), lambda g: (0, 0)),
        ],
        compiler_params=params(24),
        cost_estimate=pl.CostEstimate(flops=8 * work, bytes_accessed=4 * work, transcendentals=0),
        name="prepare",
    )(
        own,
        legendre_hi.transpose(0, 2, 1),
        legendre_lo.transpose(0, 2, 1),
        beam_weights.reshape(1, degree_count),
    )
    synthesised = pl.pallas_call(
        harmonic_kernel,
        out_shape=struct((low_rows, cols), BF16),
        in_specs=[vmem()] * 6,
        out_specs=vmem(),
        scratch_shapes=[pltpu.VMEM((owned * low_total, cols), BF16)],
        compiler_params=params(16),
        name="harmonic",
    )(received.reshape(rows, cols), gather, scatter, hi_table, lo_table, weights)
    returned = lax.all_to_all(
        synthesised.reshape(devices, owned * low_pairs, cols),
        axes,
        split_axis=0,
        concat_axis=0,
        tiled=True,
    )

    blocks_lo = NPIX_LO // (F32_ROWS // HEMIS * LANES)
    side = LANES * low_pairs
    inverse_table, regroup = pl.pallas_call(
        functools.partial(inverse_table_kernel, low_pairs),
        out_shape=[struct((2 * count, blocks_lo * LANES), BF16), struct((side, side), BF16)],
        in_specs=[vmem()],
        out_specs=[vmem(), vmem()],
        compiler_params=params(8),
        cost_estimate=pl.CostEstimate(
            flops=64 * count * blocks_lo * LANES,
            bytes_accessed=8 * count * blocks_lo * LANES,
            transcendentals=0,
        ),
        name="inverse_table",
    )(order_column)
    steps = 4
    wide = blocks_lo // steps
    buffer = pltpu.VMEM((map_count, low_pairs, wide, F32_ROWS, LANES), F32)
    spectrum = pltpu.VMEM((map_count * low_pairs * F32_ROWS, 2 * count), BF16)
    pixels = pl.pallas_call(
        synthesise_kernel,
        out_shape=struct((map_count, low_pairs, blocks_lo, F32_ROWS, LANES), F32),
        in_specs=[smem(), vmem(), vmem(), vmem(), vmem()],
        out_specs=hbm(),
        scratch_shapes=[
            pltpu.VMEM((low_pairs, cols, count), F32),
            spectrum,
            spectrum,
            buffer,
            buffer,
            buffer,
            buffer,
            pltpu.SemaphoreType.DMA((steps,)),
        ],
        compiler_params=params(32),
        name="synthesise",
    )(lo_cycles, order_row, inverse_table, regroup, returned.reshape(low_rows, cols))
    pixels = pixels.reshape(map_count, low_pairs, blocks_lo, F32_ROWS // HEMIS, HEMIS, LANES)
    pixels = pixels.transpose(0, 1, 4, 2, 3, 5)
    return pixels.reshape(map_count, low_pairs, HEMIS, NPIX_LO)


def solution(mesh):
    spread = ("band", "ma")
    return jax.shard_map(
        per_device,
        mesh=mesh,
        in_specs=(
            P(None, spread, None, None),
            P(spread),
            P(spread),
            P(),
            P(spread, None, None),
            P(spread, None, None),
            P(),
        ),
        out_specs=P(None, spread, None, None),
        check_vma=False,
    )
```

```python
import functools
import math

import jax
import jax.numpy as jnp
from jax import lax
from jax.experimental import pallas as pl
from jax.experimental.pallas import tpu as pltpu
from jax.sharding import PartitionSpec as P

NSIDE_HI = 4096
NSIDE_LO = 1024
NPIX_HI = 16384
NPIX_LO = 4096

LANES = 128
HEMIS = 2
BF16_ROWS = 16
WHOLE_VMEM = 67_043_328
F32_ROWS = 8
F32 = jnp.float32
BF16 = jnp.bfloat16


def unit_circle(steps, length):
    quarter = length // 4
    quadrant = (steps + quarter // 2) // quarter
    rest = steps - quadrant * quarter
    angle = rest.astype(F32) * (2.0 * math.pi / length)
    square = angle * angle
    sine = square * (1.0 / 362880.0) - 1.0 / 5040.0
    sine = square * sine + 1.0 / 120.0
    sine = square * sine - 1.0 / 6.0
    sine = angle + angle * (square * sine)
    cosine = square * (-1.0 / 3628800.0) + 1.0 / 40320.0
    cosine = square * cosine - 1.0 / 720.0
    cosine = square * cosine + 1.0 / 24.0
    cosine = square * cosine - 0.5
    cosine = 1.0 + square * cosine
    odd = (quadrant & 1) == 1
    big = jnp.where(odd, sine, cosine)
    small = jnp.where(odd, cosine, sine)
    cos_out = jnp.where(((quadrant + 1) & 2) == 2, -big, big)
    sin_out = jnp.where((quadrant & 2) == 2, -small, small)
    return cos_out, sin_out


def iota(shape, dim):
    return lax.broadcasted_iota(jnp.int32, shape, dim)


def split(value):
    high = value.astype(BF16)
    return high, (value - high.astype(F32)).astype(BF16)


def one_hot(shape, match):
    return jnp.where(match(iota(shape, 0), iota(shape, 1)), 1.0, 0.0).astype(BF16)


def dot_tn(lhs, rhs):
    return lax.dot_general(lhs, rhs, (((0,), (0,)), ((), ())), preferred_element_type=F32)


def dot_nt(lhs, rhs):
    return lax.dot_general(lhs, rhs, (((1,), (1,)), ((), ())), preferred_element_type=F32)


def dot_nn(lhs, rhs):
    return jnp.dot(lhs, rhs, preferred_element_type=F32)


def pair_rows(pairs):
    side = LANES * pairs
    return one_hot((side, side), lambda i, j: i == j % LANES * pairs + j // LANES)


def analyse_kernel(
    spans, hi_hbm, orders_hbm, sky_hbm, out_ref, hi, orders_ref, sky, table, raw_a, raw_b, sums, sems
):
    raws = (raw_a, raw_b)
    blocks = sky.shape[1]
    pairs = hi.shape[0]
    count = orders_ref.shape[1]
    map_count = sky.shape[0] // pairs
    inner = BF16_ROWS // HEMIS
    small = [
        pltpu.make_async_copy(orders_hbm, orders_ref, sems.at[0]),
        pltpu.make_async_copy(hi_hbm, hi, sems.at[1]),
    ]
    copies = []
    for c, (start, size) in enumerate(spans):
        part = pl.ds(start * pairs, size * pairs)
        copies.append(pltpu.make_async_copy(sky_hbm.at[part], sky.at[part], sems.at[2 + c]))
    for copy in small + copies:
        copy.start()

    gather = pair_rows(pairs)
    for copy in small:
        copy.wait()
    orders = orders_ref[...]
    cos_l, sin_l = unit_circle(orders * iota((LANES, count), 0) & (NPIX_HI - 1), NPIX_HI)
    stride = inner * LANES
    cos_a, sin_a = unit_circle(
        orders * (stride * iota((blocks, count), 0)) & (NPIX_HI - 1), NPIX_HI
    )
    scale = 1.0 / math.sqrt(NPIX_HI)
    cos_p, sin_p = [], []
    for p in range(pairs):
        offset = (hi[p] - NSIDE_HI + 1) & 1
        step = 2 * LANES * (iota((BF16_ROWS, count), 0) // HEMIS) + offset
        cosine, sine = unit_circle(orders * step & (2 * NPIX_HI - 1), 2 * NPIX_HI)
        cos_p.append(cosine * scale)
        sin_p.append(sine * scale)
    copies[0].wait()
    for a in range(blocks):
        ca, sa = cos_a[a : a + 1], sin_a[a : a + 1]
        table[a * LANES : (a + 1) * LANES, :count] = (ca * cos_l - sa * sin_l).astype(BF16)
        table[a * LANES : (a + 1) * LANES, count:] = (sa * cos_l + ca * sin_l).astype(BF16)

    def contract(c):
        start, size = spans[c]
        part = slice(start * pairs, (start + size) * pairs)
        rows = jnp.concatenate(
            [sky[part, a].reshape(size * pairs * BF16_ROWS, LANES) for a in range(blocks)], axis=1
        )
        half = blocks * LANES // 2
        raw = dot_nn(rows[:, :half], table[:half]) + dot_nn(rows[:, half:], table[half:])
        raws[c % 2][: size * pairs * BF16_ROWS] = raw

    sub = iota((1, F32_ROWS, count), 1)

    def sum_blocks(value):
        value = value[:, :F32_ROWS] + value[:, F32_ROWS:]
        low, high = value[:4], value[4:]
        first = sub < 4
        value = jnp.where(first, low, high) + pltpu.roll(jnp.where(first, high, low), 4, 1)
        low, high = value[:2], value[2:]
        first = (sub & 2) == 0
        value = jnp.where(first, low + pltpu.roll(low, 6, 1), high + pltpu.roll(high, 2, 1))
        low, high = value[:1], value[1:]
        first = (sub & 1) == 0
        north = jnp.where(first, low, pltpu.roll(high, 1, 1))
        south = jnp.where(first, pltpu.roll(low, 7, 1), high)
        return north[0], south[0]

    def finish(c):
        start, size = spans[c]
        rows = 8 * pairs * BF16_ROWS
        for group in range(size // 8):
            raw = raws[c % 2][group * rows : (group + 1) * rows]
            raw = raw.reshape(8, pairs, BF16_ROWS, 2 * count)
            at = start + group * 8
            for p in range(pairs):
                raw_c, raw_s = raw[:, p, :, :count], raw[:, p, :, count:]
                cosine, sine = cos_p[p][None], sin_p[p][None]
                real = sum_blocks(raw_c * cosine - raw_s * sine)
                imag = sum_blocks(raw_c * sine + raw_s * cosine)
                for h in range(HEMIS):
                    sums[p, h, 0, at : at + 8] = real[h]
                    sums[p, h, 1, at : at + 8] = -imag[h]

    contract(0)
    for c in range(1, len(spans)):
        copies[c].wait()
        contract(c)
        finish(c - 1)
    finish(len(spans) - 1)
    cols = HEMIS * 2 * map_count
    for j in range(count // LANES):
        lanes = slice(j * LANES, (j + 1) * LANES)
        held = [sums[p, :, :, :, lanes].reshape(cols, LANES).astype(BF16) for p in range(pairs)]
        block = dot_nt(gather, jnp.concatenate(held, axis=1))
        out_ref[j * LANES * pairs : (j + 1) * LANES * pairs] = block.astype(BF16)


def inverse_table_kernel(
    pairs, lo_ref, orders_ref, column_ref, table_ref, gather_ref, phase_ref
):
    count = column_ref.shape[0]
    orders = orders_ref[...]
    scale = math.sqrt(2.0 / count)
    for p in range(pairs):
        offset = (lo_ref[p] - NSIDE_LO + 1) & 1
        step = 2 * LANES * (iota((F32_ROWS, count), 0) // HEMIS) + offset
        cosine, sine = unit_circle(orders * step & (2 * NPIX_LO - 1), 2 * NPIX_LO)
        phase_ref[p, 0] = cosine * scale
        phase_ref[p, 1] = sine * scale
    column = column_ref[...]
    step = F32_ROWS // HEMIS * LANES
    cosine, sine = unit_circle(column * iota((count, LANES), 1) & (NPIX_LO - 1), NPIX_LO)
    cos_step, sin_step = unit_circle(
        jnp.broadcast_to(column * step & (NPIX_LO - 1), (count, LANES)), NPIX_LO
    )
    for a in range(table_ref.shape[1] // LANES):
        lanes = slice(a * LANES, (a + 1) * LANES)
        table_ref[:count, lanes] = cosine.astype(BF16)
        table_ref[count:, lanes] = (-sine).astype(BF16)
        cosine, sine = (
            cosine * cos_step - sine * sin_step,
            sine * cos_step + cosine * sin_step,
        )
    gather_ref[...] = pair_rows(pairs)


def slot_rows(owned, pairs, pair_total):
    shape = (pair_total * owned, owned * pair_total)
    column = iota((1, shape[1]), 1)
    slot, pair = column // pair_total, column % pair_total
    home = (pair // pairs * owned + slot) * pairs + pair % pairs
    return jnp.where(iota(shape, 0) == home, 1.0, 0.0).astype(BF16)


def prepare_kernel(pairs, own_ref, beam_ref, weight_ref, sign_ref, gather_ref):
    degrees = iota(beam_ref.shape, 1)
    for g in range(weight_ref.shape[0]):
        order = own_ref[g]
        weight_ref[g] = jnp.where(degrees >= order, beam_ref[...], 0.0)
        sign_ref[g] = (1 - 2 * ((degrees + order) & 1)).astype(F32).astype(BF16)
    owned = weight_ref.shape[0]
    gather_ref[...] = slot_rows(owned, pairs, gather_ref.shape[0] // owned)


def harmonic_kernel(
    same, pairs, low_pairs, received_ref, weight_ref, sign_ref, gather_ref, hi_hbm, lo_hbm,
    out_ref, hi_ref, lo_ref, held, sems,
):
    owned, pair_total = hi_ref.shape[:2]
    low_total = lo_ref.shape[1]
    half = received_ref.shape[1] // HEMIS
    copies = []
    for g in range(owned):
        copies.append(
            [
                pltpu.make_async_copy(source.at[g], target.at[g], sems.at[k, g])
                for k, (source, target) in enumerate(((hi_hbm, hi_ref), (lo_hbm, lo_ref)))
            ]
        )
        for copy in copies[g]:
            copy.start()
    north = dot_tn(received_ref[:, :half], gather_ref[...])
    south = dot_tn(received_ref[:, half:], gather_ref[...])
    for g in range(owned):
        lanes = slice(g * pair_total, (g + 1) * pair_total)
        coeffs = jnp.concatenate([north[:, lanes], south[:, lanes]], axis=1).astype(BF16)
        for copy in copies[g]:
            copy.wait()
        hi_table = jnp.concatenate([hi_ref[g], hi_ref[g] * sign_ref[g]], axis=0)
        alm = dot_nn(coeffs, hi_table) * weight_ref[g]
        lo_table = jnp.concatenate([lo_ref[g], lo_ref[g] * sign_ref[g]], axis=0)
        both = dot_nt(lo_table, jnp.concatenate(split(alm), axis=0))
        total = (both[:, :half] + both[:, half:]).astype(BF16)
        for h in range(HEMIS):
            held[g * low_total : (g + 1) * low_total, h * half : (h + 1) * half] = total[
                h * low_total : (h + 1) * low_total
            ]
    scatter = gather_ref[...] if same else slot_rows(owned, low_pairs, low_total)
    out_ref[...] = dot_nn(scatter, held[...]).astype(BF16)


def synthesise_kernel(
    phase_ref, table_ref, gather_ref, returned_ref, out_hbm,
    spectra, high, low, buf_a, buf_b, buf_c, buf_d, sems,
):
    buffers = (buf_a, buf_b, buf_c, buf_d)
    map_count, pairs, wide = buf_a.shape[:3]
    count = phase_ref.shape[3]
    for j in range(count // LANES):
        rows = slice(j * LANES * pairs, (j + 1) * LANES * pairs)
        turned = dot_tn(returned_ref[rows], gather_ref[...])
        for p in range(pairs):
            spectra[p, :, j * LANES : (j + 1) * LANES] = turned[:, p * LANES : (p + 1) * LANES]

    south = (iota((F32_ROWS, count), 0) & 1) == 1
    for p in range(pairs):
        cosine, sine = phase_ref[p, 0], phase_ref[p, 1]

        def turn(i):
            def spread(c):
                north = spectra[p, c * map_count + i : c * map_count + i + 1]
                at = (2 + c) * map_count + i
                return jnp.where(south, spectra[p, at : at + 1], north)

            real, imag = spread(0), spread(1)
            return real * cosine - imag * sine, imag * cosine + real * sine

        for i in range(0, map_count, 2):
            at = slice((p * map_count + i) * F32_ROWS, (p * map_count + i + 2) * F32_ROWS)
            for c, parts in enumerate(zip(turn(i), turn(i + 1))):
                lanes = slice(c * count, (c + 1) * count)
                high[at, lanes], low[at, lanes] = split(jnp.concatenate(parts, axis=0))

    copies = []
    for n, buffer in enumerate(buffers):
        table = table_ref[:, n * wide * LANES : (n + 1) * wide * LANES]
        pixels = dot_nn(high[...], table) + dot_nn(low[...], table)
        pixels = pixels.reshape(pairs, map_count, F32_ROWS, wide * LANES)
        for p in range(pairs):
            for a in range(wide):
                buffer[:, p, a] = pixels[p, :, :, a * LANES : (a + 1) * LANES]
        target = out_hbm.at[:, :, pl.ds(n * wide, wide)]
        copies.append(pltpu.make_async_copy(buffer, target, sems.at[n]))
        copies[-1].start()
    for copy in copies:
        copy.wait()


def vmem():
    return pl.BlockSpec(memory_space=pltpu.VMEM)


def smem():
    return pl.BlockSpec(memory_space=pltpu.SMEM)


def hbm():
    return pl.BlockSpec(memory_space=pltpu.HBM)


def params(grant=WHOLE_VMEM):
    return pltpu.CompilerParams(vmem_limit_bytes=grant)


def struct(shape, dtype):
    return jax.ShapeDtypeStruct(shape, dtype)


def per_device(
    sky_maps, hi_cycles, lo_cycles, azimuth_orders, legendre_hi, legendre_lo, beam_weights
):
    axes = ("band", "ma")
    map_count, pairs = sky_maps.shape[:2]
    low_pairs = lo_cycles.shape[0]
    count = azimuth_orders.shape[0]
    owned, degree_count, pair_total = legendre_hi.shape
    low_total = legendre_lo.shape[2]
    devices = count // owned
    order_row = azimuth_orders.reshape(1, count)
    order_column = azimuth_orders.reshape(count, 1)
    cols = HEMIS * 2 * map_count

    inner = BF16_ROWS // HEMIS
    blocks = NPIX_HI // (inner * LANES)
    sky = sky_maps.reshape(map_count, pairs, HEMIS, blocks, inner, LANES)
    sky = sky.transpose(0, 1, 3, 4, 2, 5)
    sky = sky.reshape(map_count * pairs, blocks, BF16_ROWS, LANES)
    quarter = map_count // 4
    spans = [(k * quarter, quarter) for k in range(3)]
    spans += [(3 * quarter, quarter // 2), (3 * quarter + quarter // 2, quarter // 2)]
    raw = pltpu.VMEM((quarter * pairs * BF16_ROWS, 2 * count), F32)
    outgoing = pl.pallas_call(
        functools.partial(analyse_kernel, spans),
        out_shape=struct((count * pairs, cols), BF16),
        in_specs=[hbm(), hbm(), hbm()],
        out_specs=vmem(),
        scratch_shapes=[
            pltpu.SMEM((pairs,), jnp.int32),
            pltpu.VMEM((1, count), jnp.int32),
            pltpu.VMEM((map_count * pairs, blocks, BF16_ROWS, LANES), BF16),
            pltpu.VMEM((blocks * LANES, 2 * count), BF16),
            raw,
            raw,
            pltpu.VMEM((pairs, HEMIS, 2, map_count, count), F32),
            pltpu.SemaphoreType.DMA((2 + len(spans),)),
        ],
        compiler_params=params(),
        name="analyse",
    )(hi_cycles, order_row, sky)
    received = lax.all_to_all(
        outgoing.reshape(devices, owned * pairs, cols), axes, split_axis=0, concat_axis=0, tiled=True
    )

    rows = count * pairs
    own = lax.dynamic_slice_in_dim(azimuth_orders, lax.axis_index(axes) * owned, owned)
    low_rows = count * low_pairs
    same = (low_pairs, low_total) == (pairs, pair_total)
    weights, signs, gather = pl.pallas_call(
        functools.partial(prepare_kernel, pairs),
        out_shape=[
            struct((owned, 1, degree_count), F32),
            struct((owned, 1, degree_count), BF16),
            struct((rows, owned * pair_total), BF16),
        ],
        in_specs=[smem(), vmem()],
        out_specs=[vmem()] * 3,
        compiler_params=params(16 * 2**20),
        cost_estimate=pl.CostEstimate(
            flops=2**10 * degree_count, bytes_accessed=2**10 * degree_count, transcendentals=0
        ),
        name="prepare",
    )(own, beam_weights.reshape(1, degree_count))
    synthesised = pl.pallas_call(
        functools.partial(harmonic_kernel, same, pairs, low_pairs),
        out_shape=struct((low_rows, cols), BF16),
        in_specs=[vmem(), vmem(), vmem(), vmem(), hbm(), hbm()],
        out_specs=vmem(),
        scratch_shapes=[
            pltpu.VMEM((owned, pair_total, degree_count), BF16),
            pltpu.VMEM((owned, low_total, degree_count), BF16),
            pltpu.VMEM((owned * low_total, cols), BF16),
            pltpu.SemaphoreType.DMA((2, owned)),
        ],
        compiler_params=params(52 * 2**20),
        name="harmonic",
    )(
        received.reshape(rows, cols),
        weights,
        signs,
        gather,
        legendre_hi.transpose(0, 2, 1),
        legendre_lo.transpose(0, 2, 1),
    )
    returned = lax.all_to_all(
        synthesised.reshape(devices, owned * low_pairs, cols),
        axes,
        split_axis=0,
        concat_axis=0,
        tiled=True,
    )

    blocks_lo = NPIX_LO // (F32_ROWS // HEMIS * LANES)
    side = LANES * low_pairs
    inverse_table, regroup, phase = pl.pallas_call(
        functools.partial(inverse_table_kernel, low_pairs),
        out_shape=[
            struct((2 * count, blocks_lo * LANES), BF16),
            struct((side, side), BF16),
            struct((low_pairs, 2, F32_ROWS, count), F32),
        ],
        in_specs=[smem(), vmem(), vmem()],
        out_specs=[vmem()] * 3,
        compiler_params=params(8 * 2**20),
        cost_estimate=pl.CostEstimate(
            flops=64 * count * blocks_lo * LANES,
            bytes_accessed=8 * count * blocks_lo * LANES,
            transcendentals=0,
        ),
        name="inverse_table",
    )(lo_cycles, order_row, order_column)
    steps = 4
    wide = blocks_lo // steps
    buffer = pltpu.VMEM((map_count, low_pairs, wide, F32_ROWS, LANES), F32)
    spectrum = pltpu.VMEM((map_count * low_pairs * F32_ROWS, 2 * count), BF16)
    pixels = pl.pallas_call(
        synthesise_kernel,
        out_shape=struct((map_count, low_pairs, blocks_lo, F32_ROWS, LANES), F32),
        in_specs=[vmem(), vmem(), vmem(), vmem()],
        out_specs=hbm(),
        scratch_shapes=[
            pltpu.VMEM((low_pairs, cols, count), F32),
            spectrum,
            spectrum,
            buffer,
            buffer,
            buffer,
            buffer,
            pltpu.SemaphoreType.DMA((steps,)),
        ],
        compiler_params=params(32 * 2**20),
        name="synthesise",
    )(phase, inverse_table, regroup, returned.reshape(low_rows, cols))
    pixels = pixels.reshape(map_count, low_pairs, blocks_lo, F32_ROWS // HEMIS, HEMIS, LANES)
    pixels = pixels.transpose(0, 1, 4, 2, 3, 5)
    return pixels.reshape(map_count, low_pairs, HEMIS, NPIX_LO)


def solution(mesh):
    spread = ("band", "ma")
    return jax.shard_map(
        per_device,
        mesh=mesh,
        in_specs=(
            P(None, spread, None, None),
            P(spread),
            P(spread),
            P(),
            P(spread, None, None),
            P(spread, None, None),
            P(),
        ),
        out_specs=P(None, spread, None, None),
        check_vma=False,
    )
```

```python
import functools
import math

import jax
import jax.numpy as jnp
from jax import lax
from jax.experimental import pallas as pl
from jax.experimental.pallas import tpu as pltpu
from jax.sharding import PartitionSpec as P

NSIDE_HI = 4096
NSIDE_LO = 1024
NPIX_HI = 16384
NPIX_LO = 4096

LANES = 128
HEMIS = 2
BF16_ROWS = 16
WHOLE_VMEM = 67_043_328
F32_ROWS = 8
F32 = jnp.float32
BF16 = jnp.bfloat16


def unit_circle(steps, length):
    quarter = length // 4
    quadrant = (steps + quarter // 2) // quarter
    rest = steps - quadrant * quarter
    angle = rest.astype(F32) * (2.0 * math.pi / length)
    square = angle * angle
    sine = square * (1.0 / 362880.0) - 1.0 / 5040.0
    sine = square * sine + 1.0 / 120.0
    sine = square * sine - 1.0 / 6.0
    sine = angle + angle * (square * sine)
    cosine = square * (-1.0 / 3628800.0) + 1.0 / 40320.0
    cosine = square * cosine - 1.0 / 720.0
    cosine = square * cosine + 1.0 / 24.0
    cosine = square * cosine - 0.5
    cosine = 1.0 + square * cosine
    odd = (quadrant & 1) == 1
    big = jnp.where(odd, sine, cosine)
    small = jnp.where(odd, cosine, sine)
    cos_out = jnp.where(((quadrant + 1) & 2) == 2, -big, big)
    sin_out = jnp.where((quadrant & 2) == 2, -small, small)
    return cos_out, sin_out


def iota(shape, dim):
    return lax.broadcasted_iota(jnp.int32, shape, dim)


def split(value):
    high = value.astype(BF16)
    return high, (value - high.astype(F32)).astype(BF16)


def one_hot(shape, match):
    return jnp.where(match(iota(shape, 0), iota(shape, 1)), 1.0, 0.0).astype(BF16)


def dot_tn(lhs, rhs):
    return lax.dot_general(lhs, rhs, (((0,), (0,)), ((), ())), preferred_element_type=F32)


def dot_nt(lhs, rhs):
    return lax.dot_general(lhs, rhs, (((1,), (1,)), ((), ())), preferred_element_type=F32)


def dot_nn(lhs, rhs):
    return jnp.dot(lhs, rhs, preferred_element_type=F32)


def pair_rows(pairs):
    side = LANES * pairs
    return one_hot((side, side), lambda i, j: i == j % LANES * pairs + j // LANES)


def analyse_kernel(
    spans, hi_hbm, orders_hbm, sky_hbm, out_ref, hi, orders_ref, sky, table, raw_a, raw_b, sums, sems
):
    raws = (raw_a, raw_b)
    blocks = sky.shape[1]
    pairs = hi.shape[0]
    count = orders_ref.shape[1]
    map_count = sky.shape[0] // pairs
    inner = BF16_ROWS // HEMIS
    small = [
        pltpu.make_async_copy(orders_hbm, orders_ref, sems.at[0]),
        pltpu.make_async_copy(hi_hbm, hi, sems.at[1]),
    ]
    copies = []
    for c, (start, size) in enumerate(spans):
        part = pl.ds(start * pairs, size * pairs)
        copies.append(pltpu.make_async_copy(sky_hbm.at[part], sky.at[part], sems.at[2 + c]))
    for copy in small + copies:
        copy.start()

    gather = pair_rows(pairs)
    for copy in small:
        copy.wait()
    orders = orders_ref[...]
    cos_l, sin_l = unit_circle(orders * iota((LANES, count), 0) & (NPIX_HI - 1), NPIX_HI)
    stride = inner * LANES
    cos_a, sin_a = unit_circle(
        orders * (stride * iota((blocks, count), 0)) & (NPIX_HI - 1), NPIX_HI
    )
    scale = 1.0 / math.sqrt(NPIX_HI)
    cos_p, sin_p = [], []
    for p in range(pairs):
        offset = (hi[p] - NSIDE_HI + 1) & 1
        step = 2 * LANES * (iota((BF16_ROWS, count), 0) // HEMIS) + offset
        cosine, sine = unit_circle(orders * step & (2 * NPIX_HI - 1), 2 * NPIX_HI)
        cos_p.append(cosine * scale)
        sin_p.append(sine * scale)
    copies[0].wait()
    for a in range(blocks):
        ca, sa = cos_a[a : a + 1], sin_a[a : a + 1]
        table[a * LANES : (a + 1) * LANES, :count] = (ca * cos_l - sa * sin_l).astype(BF16)
        table[a * LANES : (a + 1) * LANES, count:] = (sa * cos_l + ca * sin_l).astype(BF16)

    def contract(c):
        start, size = spans[c]
        part = slice(start * pairs, (start + size) * pairs)
        rows = jnp.concatenate(
            [sky[part, a].reshape(size * pairs * BF16_ROWS, LANES) for a in range(blocks)], axis=1
        )
        full = size * pairs * BF16_ROWS
        raws[c % 2][: full // 2] = dot_nn(rows[: full // 2], table[...])
        raws[c % 2][full // 2 : full] = dot_nn(rows[full // 2 :], table[...])

    sub = iota((1, F32_ROWS, count), 1)

    def sum_blocks(value):
        value = value[:, :F32_ROWS] + value[:, F32_ROWS:]
        low, high = value[:4], value[4:]
        first = sub < 4
        value = jnp.where(first, low, high) + pltpu.roll(jnp.where(first, high, low), 4, 1)
        low, high = value[:2], value[2:]
        first = (sub & 2) == 0
        value = jnp.where(first, low + pltpu.roll(low, 6, 1), high + pltpu.roll(high, 2, 1))
        low, high = value[:1], value[1:]
        first = (sub & 1) == 0
        north = jnp.where(first, low, pltpu.roll(high, 1, 1))
        south = jnp.where(first, pltpu.roll(low, 7, 1), high)
        return north[0], south[0]

    def finish(c):
        start, size = spans[c]
        rows = 8 * pairs * BF16_ROWS
        for group in range(size // 8):
            raw = raws[c % 2][group * rows : (group + 1) * rows]
            raw = raw.reshape(8, pairs, BF16_ROWS, 2 * count)
            at = start + group * 8
            for p in range(pairs):
                raw_c, raw_s = raw[:, p, :, :count], raw[:, p, :, count:]
                cosine, sine = cos_p[p][None], sin_p[p][None]
                real = sum_blocks(raw_c * cosine - raw_s * sine)
                imag = sum_blocks(raw_c * sine + raw_s * cosine)
                for h in range(HEMIS):
                    sums[p, h, 0, at : at + 8] = real[h]
                    sums[p, h, 1, at : at + 8] = -imag[h]

    contract(0)
    for c in range(1, len(spans)):
        copies[c].wait()
        contract(c)
        finish(c - 1)
    finish(len(spans) - 1)
    cols = HEMIS * 2 * map_count
    for j in range(count // LANES):
        lanes = slice(j * LANES, (j + 1) * LANES)
        held = [sums[p, :, :, :, lanes].reshape(cols, LANES).astype(BF16) for p in range(pairs)]
        block = dot_nt(gather, jnp.concatenate(held, axis=1))
        out_ref[j * LANES * pairs : (j + 1) * LANES * pairs] = block.astype(BF16)


def inverse_table_kernel(
    pairs, lo_ref, orders_ref, column_ref, table_ref, gather_ref, phase_ref
):
    count = column_ref.shape[0]
    orders = orders_ref[...]
    scale = math.sqrt(2.0 / count)
    for p in range(pairs):
        offset = (lo_ref[p] - NSIDE_LO + 1) & 1
        step = 2 * LANES * (iota((F32_ROWS, count), 0) // HEMIS) + offset
        cosine, sine = unit_circle(orders * step & (2 * NPIX_LO - 1), 2 * NPIX_LO)
        phase_ref[p, 0] = cosine * scale
        phase_ref[p, 1] = sine * scale
    column = column_ref[...]
    step = F32_ROWS // HEMIS * LANES
    cosine, sine = unit_circle(column * iota((count, LANES), 1) & (NPIX_LO - 1), NPIX_LO)
    cos_step, sin_step = unit_circle(
        jnp.broadcast_to(column * step & (NPIX_LO - 1), (count, LANES)), NPIX_LO
    )
    for a in range(table_ref.shape[1] // LANES):
        lanes = slice(a * LANES, (a + 1) * LANES)
        table_ref[:count, lanes] = cosine.astype(BF16)
        table_ref[count:, lanes] = (-sine).astype(BF16)
        cosine, sine = (
            cosine * cos_step - sine * sin_step,
            sine * cos_step + cosine * sin_step,
        )
    gather_ref[...] = pair_rows(pairs)


def slot_rows(owned, pairs, pair_total):
    shape = (pair_total * owned, owned * pair_total)
    column = iota((1, shape[1]), 1)
    slot, pair = column // pair_total, column % pair_total
    home = (pair // pairs * owned + slot) * pairs + pair % pairs
    return jnp.where(iota(shape, 0) == home, 1.0, 0.0).astype(BF16)


def prepare_kernel(
    pairs, own_ref, beam_ref, hi_hbm, lo_hbm, weight_ref, sign_ref, gather_ref, hi_out, lo_out, sems
):
    copies = [
        pltpu.make_async_copy(hi_hbm, hi_out, sems.at[0]),
        pltpu.make_async_copy(lo_hbm, lo_out, sems.at[1]),
    ]
    for copy in copies:
        copy.start()
    degrees = iota(beam_ref.shape, 1)
    owned = weight_ref.shape[0]
    for g in range(owned):
        order = own_ref[g]
        weight_ref[g] = jnp.where(degrees >= order, beam_ref[...], 0.0)
        sign_ref[g] = (1 - 2 * ((degrees + order) & 1)).astype(F32).astype(BF16)
    gather_ref[...] = slot_rows(owned, pairs, gather_ref.shape[0] // owned)
    for copy in copies:
        copy.wait()


def harmonic_kernel(
    same, low_pairs, received_ref, weight_ref, sign_ref, gather_ref, hi_ref, lo_ref, out_ref, held
):
    owned, pair_total = hi_ref.shape[:2]
    low_total = lo_ref.shape[1]
    half = received_ref.shape[1] // HEMIS
    north = dot_tn(received_ref[:, :half], gather_ref[...])
    south = dot_tn(received_ref[:, half:], gather_ref[...])
    for g in range(owned):
        lanes = slice(g * pair_total, (g + 1) * pair_total)
        coeffs = jnp.concatenate([north[:, lanes], south[:, lanes]], axis=1).astype(BF16)
        hi_table = jnp.concatenate([hi_ref[g], hi_ref[g] * sign_ref[g]], axis=0)
        alm = dot_nn(coeffs, hi_table) * weight_ref[g]
        lo_table = jnp.concatenate([lo_ref[g], lo_ref[g] * sign_ref[g]], axis=0)
        both = dot_nt(jnp.concatenate(split(alm), axis=0), lo_table)
        total = (both[:half] + both[half:]).T.astype(BF16)
        for h in range(HEMIS):
            held[g * low_total : (g + 1) * low_total, h * half : (h + 1) * half] = total[
                h * low_total : (h + 1) * low_total
            ]
    scatter = gather_ref[...] if same else slot_rows(owned, low_pairs, low_total)
    out_ref[...] = dot_nn(scatter, held[...]).astype(BF16)


def synthesise_kernel(
    phase_ref, table_ref, gather_ref, returned_ref, out_hbm,
    spectra, high, low, buf_a, buf_b, buf_c, buf_d, sems,
):
    buffers = (buf_a, buf_b, buf_c, buf_d)
    map_count, pairs, wide = buf_a.shape[:3]
    count = phase_ref.shape[3]
    for j in range(count // LANES):
        rows = slice(j * LANES * pairs, (j + 1) * LANES * pairs)
        turned = dot_tn(returned_ref[rows], gather_ref[...])
        for p in range(pairs):
            spectra[p, :, j * LANES : (j + 1) * LANES] = turned[:, p * LANES : (p + 1) * LANES]

    south = (iota((F32_ROWS, count), 0) & 1) == 1
    for p in range(pairs):
        cosine, sine = phase_ref[p, 0], phase_ref[p, 1]

        def turn(i):
            def spread(c):
                north = spectra[p, c * map_count + i : c * map_count + i + 1]
                at = (2 + c) * map_count + i
                return jnp.where(south, spectra[p, at : at + 1], north)

            real, imag = spread(0), spread(1)
            return real * cosine - imag * sine, imag * cosine + real * sine

        for i in range(0, map_count, 2):
            at = slice((p * map_count + i) * F32_ROWS, (p * map_count + i + 2) * F32_ROWS)
            for c, parts in enumerate(zip(turn(i), turn(i + 1))):
                lanes = slice(c * count, (c + 1) * count)
                high[at, lanes], low[at, lanes] = split(jnp.concatenate(parts, axis=0))

    copies = []
    for n, buffer in enumerate(buffers):
        table = table_ref[:, n * wide * LANES : (n + 1) * wide * LANES]
        pixels = dot_nn(high[...], table) + dot_nn(low[...], table)
        pixels = pixels.reshape(pairs, map_count, F32_ROWS, wide * LANES)
        for p in range(pairs):
            for a in range(wide):
                buffer[:, p, a] = pixels[p, :, :, a * LANES : (a + 1) * LANES]
        target = out_hbm.at[:, :, pl.ds(n * wide, wide)]
        copies.append(pltpu.make_async_copy(buffer, target, sems.at[n]))
        copies[-1].start()
    for copy in copies:
        copy.wait()


def vmem():
    return pl.BlockSpec(memory_space=pltpu.VMEM)


def smem():
    return pl.BlockSpec(memory_space=pltpu.SMEM)


def hbm():
    return pl.BlockSpec(memory_space=pltpu.HBM)


def params(grant=WHOLE_VMEM):
    return pltpu.CompilerParams(vmem_limit_bytes=grant)


def struct(shape, dtype):
    return jax.ShapeDtypeStruct(shape, dtype)


def analyse(sky_maps, hi_cycles, azimuth_orders):
    map_count, pairs = sky_maps.shape[:2]
    count = azimuth_orders.shape[0]
    cols = HEMIS * 2 * map_count
    inner = BF16_ROWS // HEMIS
    blocks = NPIX_HI // (inner * LANES)
    sky = sky_maps.reshape(map_count, pairs, HEMIS, blocks, inner, LANES)
    sky = sky.transpose(0, 1, 3, 4, 2, 5)
    sky = sky.reshape(map_count * pairs, blocks, BF16_ROWS, LANES)
    size = map_count // 4
    spans = [(k * size, size) for k in range(4)]
    raw = pltpu.VMEM((size * pairs * BF16_ROWS, 2 * count), F32)
    return pl.pallas_call(
        functools.partial(analyse_kernel, spans),
        out_shape=struct((count * pairs, cols), BF16),
        in_specs=[hbm(), hbm(), hbm()],
        out_specs=vmem(),
        scratch_shapes=[
            pltpu.SMEM((pairs,), jnp.int32),
            pltpu.VMEM((1, count), jnp.int32),
            pltpu.VMEM((map_count * pairs, blocks, BF16_ROWS, LANES), BF16),
            pltpu.VMEM((blocks * LANES, 2 * count), BF16),
            raw,
            raw,
            pltpu.VMEM((pairs, HEMIS, 2, map_count, count), F32),
            pltpu.SemaphoreType.DMA((2 + len(spans),)),
        ],
        compiler_params=params(),
        name="analyse",
    )(hi_cycles, azimuth_orders.reshape(1, count), sky)


def per_device(
    sky_maps, hi_cycles, lo_cycles, azimuth_orders, legendre_hi, legendre_lo, beam_weights
):
    axes = ("band", "ma")
    map_count, pairs = sky_maps.shape[:2]
    low_pairs = lo_cycles.shape[0]
    count = azimuth_orders.shape[0]
    owned, degree_count, pair_total = legendre_hi.shape
    low_total = legendre_lo.shape[2]
    devices = count // owned
    order_row = azimuth_orders.reshape(1, count)
    order_column = azimuth_orders.reshape(count, 1)
    cols = HEMIS * 2 * map_count

    outgoing = analyse(sky_maps, hi_cycles, azimuth_orders)
    received = lax.all_to_all(
        outgoing.reshape(devices, owned * pairs, cols), axes, split_axis=0, concat_axis=0, tiled=True
    )

    rows = count * pairs
    own = lax.dynamic_slice_in_dim(azimuth_orders, lax.axis_index(axes) * owned, owned)
    low_rows = count * low_pairs
    same = (low_pairs, low_total) == (pairs, pair_total)
    hi_blocks, lo_blocks = legendre_hi.transpose(0, 2, 1), legendre_lo.transpose(0, 2, 1)
    prepared = pl.pallas_call(
        functools.partial(prepare_kernel, pairs),
        out_shape=[
            struct((owned, 1, degree_count), F32),
            struct((owned, 1, degree_count), BF16),
            struct((rows, owned * pair_total), BF16),
            struct(hi_blocks.shape, BF16),
            struct(lo_blocks.shape, BF16),
        ],
        in_specs=[smem(), vmem(), hbm(), hbm()],
        out_specs=[vmem()] * 5,
        scratch_shapes=[pltpu.SemaphoreType.DMA((2,))],
        compiler_params=params(50 * 2**20),
        cost_estimate=pl.CostEstimate(
            flops=2**10 * degree_count, bytes_accessed=2**10 * degree_count, transcendentals=0
        ),
        name="prepare",
    )(own, beam_weights.reshape(1, degree_count), hi_blocks, lo_blocks)
    synthesised = pl.pallas_call(
        functools.partial(harmonic_kernel, same, low_pairs),
        out_shape=struct((low_rows, cols), BF16),
        in_specs=[vmem()] * 6,
        out_specs=vmem(),
        scratch_shapes=[pltpu.VMEM((owned * low_total, cols), BF16)],
        compiler_params=params(16 * 2**20),
        name="harmonic",
    )(received.reshape(rows, cols), *prepared)
    returned = lax.all_to_all(
        synthesised.reshape(devices, owned * low_pairs, cols),
        axes,
        split_axis=0,
        concat_axis=0,
        tiled=True,
    )

    blocks_lo = NPIX_LO // (F32_ROWS // HEMIS * LANES)
    side = LANES * low_pairs
    inverse_table, regroup, phase = pl.pallas_call(
        functools.partial(inverse_table_kernel, low_pairs),
        out_shape=[
            struct((2 * count, blocks_lo * LANES), BF16),
            struct((side, side), BF16),
            struct((low_pairs, 2, F32_ROWS, count), F32),
        ],
        in_specs=[smem(), vmem(), vmem()],
        out_specs=[vmem()] * 3,
        compiler_params=params(8 * 2**20),
        cost_estimate=pl.CostEstimate(
            flops=64 * count * blocks_lo * LANES,
            bytes_accessed=8 * count * blocks_lo * LANES,
            transcendentals=0,
        ),
        name="inverse_table",
    )(lo_cycles, order_row, order_column)
    steps = 4
    wide = blocks_lo // steps
    buffer = pltpu.VMEM((map_count, low_pairs, wide, F32_ROWS, LANES), F32)
    spectrum = pltpu.VMEM((map_count * low_pairs * F32_ROWS, 2 * count), BF16)
    pixels = pl.pallas_call(
        synthesise_kernel,
        out_shape=struct((map_count, low_pairs, blocks_lo, F32_ROWS, LANES), F32),
        in_specs=[vmem(), vmem(), vmem(), vmem()],
        out_specs=hbm(),
        scratch_shapes=[
            pltpu.VMEM((low_pairs, cols, count), F32),
            spectrum,
            spectrum,
            buffer,
            buffer,
            buffer,
            buffer,
            pltpu.SemaphoreType.DMA((steps,)),
        ],
        compiler_params=params(32 * 2**20),
        name="synthesise",
    )(phase, inverse_table, regroup, returned.reshape(low_rows, cols))
    pixels = pixels.reshape(map_count, low_pairs, blocks_lo, F32_ROWS // HEMIS, HEMIS, LANES)
    pixels = pixels.transpose(0, 1, 4, 2, 3, 5)
    return pixels.reshape(map_count, low_pairs, HEMIS, NPIX_LO)


def solution(mesh):
    spread = ("band", "ma")
    return jax.shard_map(
        per_device,
        mesh=mesh,
        in_specs=(
            P(None, spread, None, None),
            P(spread),
            P(spread),
            P(),
            P(spread, None, None),
            P(spread, None, None),
            P(),
        ),
        out_specs=P(None, spread, None, None),
        check_vma=False,
    )
```

```python
import functools
import math

import jax
import jax.numpy as jnp
from jax import lax
from jax.experimental import pallas as pl
from jax.experimental.pallas import tpu as pltpu
from jax.sharding import PartitionSpec as P

NSIDE_HI = 4096
NSIDE_LO = 1024
NPIX_HI = 16384
NPIX_LO = 4096

LANES = 128
HEMIS = 2
BF16_ROWS = 16
WHOLE_VMEM = 67_043_328
F32_ROWS = 8
F32 = jnp.float32
BF16 = jnp.bfloat16


def unit_circle(steps, length):
    quarter = length // 4
    quadrant = (steps + quarter // 2) // quarter
    rest = steps - quadrant * quarter
    angle = rest.astype(F32) * (2.0 * math.pi / length)
    square = angle * angle
    sine = square * (1.0 / 362880.0) - 1.0 / 5040.0
    sine = square * sine + 1.0 / 120.0
    sine = square * sine - 1.0 / 6.0
    sine = angle + angle * (square * sine)
    cosine = square * (-1.0 / 3628800.0) + 1.0 / 40320.0
    cosine = square * cosine - 1.0 / 720.0
    cosine = square * cosine + 1.0 / 24.0
    cosine = square * cosine - 0.5
    cosine = 1.0 + square * cosine
    odd = (quadrant & 1) == 1
    big = jnp.where(odd, sine, cosine)
    small = jnp.where(odd, cosine, sine)
    cos_out = jnp.where(((quadrant + 1) & 2) == 2, -big, big)
    sin_out = jnp.where((quadrant & 2) == 2, -small, small)
    return cos_out, sin_out


def iota(shape, dim):
    return lax.broadcasted_iota(jnp.int32, shape, dim)


def split(value):
    high = value.astype(BF16)
    return high, (value - high.astype(F32)).astype(BF16)


def one_hot(shape, match):
    return jnp.where(match(iota(shape, 0), iota(shape, 1)), 1.0, 0.0).astype(BF16)


def dot_tn(lhs, rhs):
    return lax.dot_general(lhs, rhs, (((0,), (0,)), ((), ())), preferred_element_type=F32)


def dot_nt(lhs, rhs):
    return lax.dot_general(lhs, rhs, (((1,), (1,)), ((), ())), preferred_element_type=F32)


def dot_nn(lhs, rhs):
    return jnp.dot(lhs, rhs, preferred_element_type=F32)


def pair_rows(pairs):
    side = LANES * pairs
    return one_hot((side, side), lambda i, j: i == j % LANES * pairs + j // LANES)


def analyse_kernel(
    spans, hi_hbm, orders_hbm, sky_hbm, out_ref, hi, orders_ref, sky, table, raw_a, raw_b, sums, sems
):
    raws = (raw_a, raw_b)
    blocks = sky.shape[1]
    pairs = hi.shape[0]
    count = orders_ref.shape[1]
    map_count = sky.shape[0] // pairs
    inner = BF16_ROWS // HEMIS
    small = [
        pltpu.make_async_copy(orders_hbm, orders_ref, sems.at[0]),
        pltpu.make_async_copy(hi_hbm, hi, sems.at[1]),
    ]
    copies = []
    for c, (start, size) in enumerate(spans):
        part = pl.ds(start * pairs, size * pairs)
        copies.append(pltpu.make_async_copy(sky_hbm.at[part], sky.at[part], sems.at[2 + c]))
    for copy in small + copies:
        copy.start()

    gather = pair_rows(pairs)
    for copy in small:
        copy.wait()
    orders = orders_ref[...]
    cos_l, sin_l = unit_circle(orders * iota((LANES, count), 0) & (NPIX_HI - 1), NPIX_HI)
    stride = inner * LANES
    cos_a, sin_a = unit_circle(
        orders * (stride * iota((blocks, count), 0)) & (NPIX_HI - 1), NPIX_HI
    )
    scale = 1.0 / math.sqrt(NPIX_HI)
    cos_p, sin_p = [], []
    for p in range(pairs):
        offset = (hi[p] - NSIDE_HI + 1) & 1
        step = 2 * LANES * (iota((BF16_ROWS, count), 0) // HEMIS) + offset
        cosine, sine = unit_circle(orders * step & (2 * NPIX_HI - 1), 2 * NPIX_HI)
        cos_p.append(cosine * scale)
        sin_p.append(sine * scale)
    copies[0].wait()
    for a in range(blocks):
        ca, sa = cos_a[a : a + 1], sin_a[a : a + 1]
        table[a * LANES : (a + 1) * LANES, :count] = (ca * cos_l - sa * sin_l).astype(BF16)
        table[a * LANES : (a + 1) * LANES, count:] = (sa * cos_l + ca * sin_l).astype(BF16)

    def contract(c):
        start, size = spans[c]
        part = slice(start * pairs, (start + size) * pairs)
        rows = jnp.concatenate(
            [sky[part, a].reshape(size * pairs * BF16_ROWS, LANES) for a in range(blocks)], axis=1
        )
        full = size * pairs * BF16_ROWS
        raws[c % 2][: full // 2] = dot_nn(rows[: full // 2], table[...])
        raws[c % 2][full // 2 : full] = dot_nn(rows[full // 2 :], table[...])

    sub = iota((1, F32_ROWS, count), 1)

    def sum_blocks(value):
        value = value[:, :F32_ROWS] + value[:, F32_ROWS:]
        low, high = value[:4], value[4:]
        first = sub < 4
        value = jnp.where(first, low, high) + pltpu.roll(jnp.where(first, high, low), 4, 1)
        low, high = value[:2], value[2:]
        first = (sub & 2) == 0
        value = jnp.where(first, low + pltpu.roll(low, 6, 1), high + pltpu.roll(high, 2, 1))
        low, high = value[:1], value[1:]
        first = (sub & 1) == 0
        north = jnp.where(first, low, pltpu.roll(high, 1, 1))
        south = jnp.where(first, pltpu.roll(low, 7, 1), high)
        return north[0], south[0]

    def finish(c):
        start, size = spans[c]
        rows = 8 * pairs * BF16_ROWS
        for group in range(size // 8):
            raw = raws[c % 2][group * rows : (group + 1) * rows]
            raw = raw.reshape(8, pairs, BF16_ROWS, 2 * count)
            at = start + group * 8
            for p in range(pairs):
                raw_c, raw_s = raw[:, p, :, :count], raw[:, p, :, count:]
                cosine, sine = cos_p[p][None], sin_p[p][None]
                real = sum_blocks(raw_c * cosine - raw_s * sine)
                imag = sum_blocks(raw_c * sine + raw_s * cosine)
                for h in range(HEMIS):
                    sums[p, h, 0, at : at + 8] = real[h]
                    sums[p, h, 1, at : at + 8] = -imag[h]

    contract(0)
    for c in range(1, len(spans)):
        copies[c].wait()
        contract(c)
        finish(c - 1)
    finish(len(spans) - 1)
    cols = HEMIS * 2 * map_count
    for j in range(count // LANES):
        lanes = slice(j * LANES, (j + 1) * LANES)
        held = [sums[p, :, :, :, lanes].reshape(cols, LANES).astype(BF16) for p in range(pairs)]
        block = dot_nt(gather, jnp.concatenate(held, axis=1))
        out_ref[j * LANES * pairs : (j + 1) * LANES * pairs] = block.astype(BF16)


def inverse_table_kernel(
    pairs, lo_ref, orders_ref, column_ref, table_ref, gather_ref, phase_ref
):
    count = column_ref.shape[0]
    orders = orders_ref[...]
    scale = math.sqrt(2.0 / count)
    for p in range(pairs):
        offset = (lo_ref[p] - NSIDE_LO + 1) & 1
        step = 2 * LANES * (iota((F32_ROWS, count), 0) // HEMIS) + offset
        cosine, sine = unit_circle(orders * step & (2 * NPIX_LO - 1), 2 * NPIX_LO)
        phase_ref[p, 0] = cosine * scale
        phase_ref[p, 1] = sine * scale
    column = column_ref[...]
    step = F32_ROWS // HEMIS * LANES
    cosine, sine = unit_circle(column * iota((count, LANES), 1) & (NPIX_LO - 1), NPIX_LO)
    cos_step, sin_step = unit_circle(
        jnp.broadcast_to(column * step & (NPIX_LO - 1), (count, LANES)), NPIX_LO
    )
    for a in range(table_ref.shape[1] // LANES):
        lanes = slice(a * LANES, (a + 1) * LANES)
        table_ref[:count, lanes] = cosine.astype(BF16)
        table_ref[count:, lanes] = (-sine).astype(BF16)
        cosine, sine = (
            cosine * cos_step - sine * sin_step,
            sine * cos_step + cosine * sin_step,
        )
    gather_ref[...] = pair_rows(pairs)


def slot_rows(owned, pairs, pair_total):
    shape = (pair_total * owned, owned * pair_total)
    column = iota((1, shape[1]), 1)
    slot, pair = column // pair_total, column % pair_total
    home = (pair // pairs * owned + slot) * pairs + pair % pairs
    return jnp.where(iota(shape, 0) == home, 1.0, 0.0).astype(BF16)


def prepare_kernel(
    pairs, own_ref, beam_ref, hi_hbm, lo_hbm, weight_ref, sign_ref, gather_ref, hi_out, lo_out, sems
):
    copies = [
        pltpu.make_async_copy(hi_hbm, hi_out, sems.at[0]),
        pltpu.make_async_copy(lo_hbm, lo_out, sems.at[1]),
    ]
    for copy in copies:
        copy.start()
    degrees = iota(beam_ref.shape, 1)
    owned = weight_ref.shape[0]
    for g in range(owned):
        order = own_ref[g]
        weight_ref[g] = jnp.where(degrees >= order, beam_ref[...], 0.0)
        sign_ref[g] = (1 - 2 * ((degrees + order) & 1)).astype(F32).astype(BF16)
    gather_ref[...] = slot_rows(owned, pairs, gather_ref.shape[0] // owned)
    for copy in copies:
        copy.wait()


def harmonic_kernel(
    same, low_pairs, received_ref, weight_ref, sign_ref, gather_ref, hi_ref, lo_ref, out_ref, held
):
    owned, pair_total = hi_ref.shape[:2]
    low_total = lo_ref.shape[1]
    half = received_ref.shape[1] // HEMIS
    north = dot_tn(received_ref[:, :half], gather_ref[...])
    south = dot_tn(received_ref[:, half:], gather_ref[...])
    for g in range(owned):
        lanes = slice(g * pair_total, (g + 1) * pair_total)
        coeffs = jnp.concatenate([north[:, lanes], south[:, lanes]], axis=1).astype(BF16)
        hi_table = jnp.concatenate([hi_ref[g], hi_ref[g] * sign_ref[g]], axis=0)
        alm = dot_nn(coeffs, hi_table) * weight_ref[g]
        lo_table = jnp.concatenate([lo_ref[g], lo_ref[g] * sign_ref[g]], axis=0)
        both = dot_nt(jnp.concatenate(split(alm), axis=0), lo_table)
        total = (both[:half] + both[half:]).T.astype(BF16)
        for h in range(HEMIS):
            held[g * low_total : (g + 1) * low_total, h * half : (h + 1) * half] = total[
                h * low_total : (h + 1) * low_total
            ]
    scatter = gather_ref[...] if same else slot_rows(owned, low_pairs, low_total)
    out_ref[...] = dot_nn(scatter, held[...]).astype(BF16)


def synthesise_kernel(
    phase_ref, table_ref, gather_ref, returned_ref, out_hbm, spectra, high, low, buffer, sems
):
    pairs, steps, map_count, wide = buffer.shape[:4]
    count = phase_ref.shape[3]
    for j in range(count // LANES):
        rows = slice(j * LANES * pairs, (j + 1) * LANES * pairs)
        turned = dot_tn(returned_ref[rows], gather_ref[...])
        for p in range(pairs):
            spectra[p, :, j * LANES : (j + 1) * LANES] = turned[:, p * LANES : (p + 1) * LANES]

    south = (iota((F32_ROWS, count), 0) & 1) == 1

    def turn(p, i):
        def spread(c):
            north = spectra[p, c * map_count + i : c * map_count + i + 1]
            at = (2 + c) * map_count + i
            return jnp.where(south, spectra[p, at : at + 1], north)

        real, imag = spread(0), spread(1)
        cosine, sine = phase_ref[p, 0], phase_ref[p, 1]
        return real * cosine - imag * sine, imag * cosine + real * sine

    def rotate(p, first, last):
        for i in range(first, last, 2):
            at = slice((p * map_count + i) * F32_ROWS, (p * map_count + i + 2) * F32_ROWS)
            for c, parts in enumerate(zip(turn(p, i), turn(p, i + 1))):
                lanes = slice(c * count, (c + 1) * count)
                high[at, lanes], low[at, lanes] = split(jnp.concatenate(parts, axis=0))

    copies = []
    rotate(0, 0, map_count)
    for p in range(pairs):
        rows = slice(p * map_count * F32_ROWS, (p + 1) * map_count * F32_ROWS)
        for n in range(steps):
            table = table_ref[:, n * wide * LANES : (n + 1) * wide * LANES]
            pixels = dot_nn(high[rows], table) + dot_nn(low[rows], table)
            if p + 1 < pairs:
                share = map_count // steps
                rotate(p + 1, n * share, (n + 1) * share)
            pixels = pixels.reshape(map_count, F32_ROWS, wide * LANES)
            for a in range(wide):
                buffer[p, n, :, a] = pixels[:, :, a * LANES : (a + 1) * LANES]
            target = out_hbm.at[:, p, pl.ds(n * wide, wide)]
            copies.append(pltpu.make_async_copy(buffer.at[p, n], target, sems.at[p, n]))
            copies[-1].start()
    for copy in copies:
        copy.wait()


def vmem():
    return pl.BlockSpec(memory_space=pltpu.VMEM)


def smem():
    return pl.BlockSpec(memory_space=pltpu.SMEM)


def hbm():
    return pl.BlockSpec(memory_space=pltpu.HBM)


def params(grant=WHOLE_VMEM):
    return pltpu.CompilerParams(vmem_limit_bytes=grant)


def struct(shape, dtype):
    return jax.ShapeDtypeStruct(shape, dtype)


def analyse(sky_maps, hi_cycles, azimuth_orders):
    map_count, pairs = sky_maps.shape[:2]
    count = azimuth_orders.shape[0]
    cols = HEMIS * 2 * map_count
    inner = BF16_ROWS // HEMIS
    blocks = NPIX_HI // (inner * LANES)
    sky = sky_maps.reshape(map_count, pairs, HEMIS, blocks, inner, LANES)
    sky = sky.transpose(0, 1, 3, 4, 2, 5)
    sky = sky.reshape(map_count * pairs, blocks, BF16_ROWS, LANES)
    size = map_count // 4
    spans = [(k * size, size) for k in range(4)]
    raw = pltpu.VMEM((size * pairs * BF16_ROWS, 2 * count), F32)
    return pl.pallas_call(
        functools.partial(analyse_kernel, spans),
        out_shape=struct((count * pairs, cols), BF16),
        in_specs=[hbm(), hbm(), hbm()],
        out_specs=vmem(),
        scratch_shapes=[
            pltpu.SMEM((pairs,), jnp.int32),
            pltpu.VMEM((1, count), jnp.int32),
            pltpu.VMEM((map_count * pairs, blocks, BF16_ROWS, LANES), BF16),
            pltpu.VMEM((blocks * LANES, 2 * count), BF16),
            raw,
            raw,
            pltpu.VMEM((pairs, HEMIS, 2, map_count, count), F32),
            pltpu.SemaphoreType.DMA((2 + len(spans),)),
        ],
        compiler_params=params(),
        name="analyse",
    )(hi_cycles, azimuth_orders.reshape(1, count), sky)


def per_device(
    sky_maps, hi_cycles, lo_cycles, azimuth_orders, legendre_hi, legendre_lo, beam_weights
):
    axes = ("band", "ma")
    map_count, pairs = sky_maps.shape[:2]
    low_pairs = lo_cycles.shape[0]
    count = azimuth_orders.shape[0]
    owned, degree_count, pair_total = legendre_hi.shape
    low_total = legendre_lo.shape[2]
    devices = count // owned
    order_row = azimuth_orders.reshape(1, count)
    order_column = azimuth_orders.reshape(count, 1)
    cols = HEMIS * 2 * map_count

    outgoing = analyse(sky_maps, hi_cycles, azimuth_orders)
    received = lax.all_to_all(
        outgoing.reshape(devices, owned * pairs, cols), axes, split_axis=0, concat_axis=0, tiled=True
    )

    rows = count * pairs
    own = lax.dynamic_slice_in_dim(azimuth_orders, lax.axis_index(axes) * owned, owned)
    low_rows = count * low_pairs
    same = (low_pairs, low_total) == (pairs, pair_total)
    hi_blocks, lo_blocks = legendre_hi.transpose(0, 2, 1), legendre_lo.transpose(0, 2, 1)
    prepared = pl.pallas_call(
        functools.partial(prepare_kernel, pairs),
        out_shape=[
            struct((owned, 1, degree_count), F32),
            struct((owned, 1, degree_count), BF16),
            struct((rows, owned * pair_total), BF16),
            struct(hi_blocks.shape, BF16),
            struct(lo_blocks.shape, BF16),
        ],
        in_specs=[smem(), vmem(), hbm(), hbm()],
        out_specs=[vmem()] * 5,
        scratch_shapes=[pltpu.SemaphoreType.DMA((2,))],
        compiler_params=params(50 * 2**20),
        cost_estimate=pl.CostEstimate(
            flops=2**10 * degree_count, bytes_accessed=2**10 * degree_count, transcendentals=0
        ),
        name="prepare",
    )(own, beam_weights.reshape(1, degree_count), hi_blocks, lo_blocks)
    synthesised = pl.pallas_call(
        functools.partial(harmonic_kernel, same, low_pairs),
        out_shape=struct((low_rows, cols), BF16),
        in_specs=[vmem()] * 6,
        out_specs=vmem(),
        scratch_shapes=[pltpu.VMEM((owned * low_total, cols), BF16)],
        compiler_params=params(16 * 2**20),
        name="harmonic",
    )(received.reshape(rows, cols), *prepared)
    returned = lax.all_to_all(
        synthesised.reshape(devices, owned * low_pairs, cols),
        axes,
        split_axis=0,
        concat_axis=0,
        tiled=True,
    )

    blocks_lo = NPIX_LO // (F32_ROWS // HEMIS * LANES)
    side = LANES * low_pairs
    inverse_table, regroup, phase = pl.pallas_call(
        functools.partial(inverse_table_kernel, low_pairs),
        out_shape=[
            struct((2 * count, blocks_lo * LANES), BF16),
            struct((side, side), BF16),
            struct((low_pairs, 2, F32_ROWS, count), F32),
        ],
        in_specs=[smem(), vmem(), vmem()],
        out_specs=[vmem()] * 3,
        compiler_params=params(8 * 2**20),
        cost_estimate=pl.CostEstimate(
            flops=64 * count * blocks_lo * LANES,
            bytes_accessed=8 * count * blocks_lo * LANES,
            transcendentals=0,
        ),
        name="inverse_table",
    )(lo_cycles, order_row, order_column)
    steps = 2
    wide = blocks_lo // steps
    buffer = pltpu.VMEM((low_pairs, steps, map_count, wide, F32_ROWS, LANES), F32)
    spectrum = pltpu.VMEM((map_count * low_pairs * F32_ROWS, 2 * count), BF16)
    pixels = pl.pallas_call(
        synthesise_kernel,
        out_shape=struct((map_count, low_pairs, blocks_lo, F32_ROWS, LANES), F32),
        in_specs=[vmem(), vmem(), vmem(), vmem()],
        out_specs=hbm(),
        scratch_shapes=[
            pltpu.VMEM((low_pairs, cols, count), F32),
            spectrum,
            spectrum,
            buffer,
            pltpu.SemaphoreType.DMA((low_pairs, steps)),
        ],
        compiler_params=params(32 * 2**20),
        name="synthesise",
    )(phase, inverse_table, regroup, returned.reshape(low_rows, cols))
    pixels = pixels.reshape(map_count, low_pairs, blocks_lo, F32_ROWS // HEMIS, HEMIS, LANES)
    pixels = pixels.transpose(0, 1, 4, 2, 3, 5)
    return pixels.reshape(map_count, low_pairs, HEMIS, NPIX_LO)


def solution(mesh):
    spread = ("band", "ma")
    return jax.shard_map(
        per_device,
        mesh=mesh,
        in_specs=(
            P(None, spread, None, None),
            P(spread),
            P(spread),
            P(),
            P(spread, None, None),
            P(spread, None, None),
            P(),
        ),
        out_specs=P(None, spread, None, None),
        check_vma=False,
    )
```

```python
import functools
import math

import jax
import jax.numpy as jnp
from jax import lax
from jax.experimental import pallas as pl
from jax.experimental.pallas import tpu as pltpu
from jax.sharding import PartitionSpec as P

NSIDE_HI = 4096
NSIDE_LO = 1024
NPIX_HI = 16384
NPIX_LO = 4096

LANES = 128
HEMIS = 2
BF16_ROWS = 16
WHOLE_VMEM = 67_043_328
F32_ROWS = 8
F32 = jnp.float32
BF16 = jnp.bfloat16


def unit_circle(steps, length):
    quarter = length // 4
    quadrant = (steps + quarter // 2) // quarter
    rest = steps - quadrant * quarter
    angle = rest.astype(F32) * (2.0 * math.pi / length)
    square = angle * angle
    sine = square * (1.0 / 362880.0) - 1.0 / 5040.0
    sine = square * sine + 1.0 / 120.0
    sine = square * sine - 1.0 / 6.0
    sine = angle + angle * (square * sine)
    cosine = square * (-1.0 / 3628800.0) + 1.0 / 40320.0
    cosine = square * cosine - 1.0 / 720.0
    cosine = square * cosine + 1.0 / 24.0
    cosine = square * cosine - 0.5
    cosine = 1.0 + square * cosine
    odd = (quadrant & 1) == 1
    big = jnp.where(odd, sine, cosine)
    small = jnp.where(odd, cosine, sine)
    cos_out = jnp.where(((quadrant + 1) & 2) == 2, -big, big)
    sin_out = jnp.where((quadrant & 2) == 2, -small, small)
    return cos_out, sin_out


def iota(shape, dim):
    return lax.broadcasted_iota(jnp.int32, shape, dim)


def split(value):
    high = value.astype(BF16)
    return high, (value - high.astype(F32)).astype(BF16)


def one_hot(shape, match):
    return jnp.where(match(iota(shape, 0), iota(shape, 1)), 1.0, 0.0).astype(BF16)


def dot_tn(lhs, rhs):
    return lax.dot_general(lhs, rhs, (((0,), (0,)), ((), ())), preferred_element_type=F32)


def dot_nt(lhs, rhs):
    return lax.dot_general(lhs, rhs, (((1,), (1,)), ((), ())), preferred_element_type=F32)


def dot_nn(lhs, rhs):
    return jnp.dot(lhs, rhs, preferred_element_type=F32)


def pair_rows(pairs):
    side = LANES * pairs
    return one_hot((side, side), lambda i, j: i == j % LANES * pairs + j // LANES)


def analyse_kernel(
    spans, hi_hbm, orders_hbm, sky_hbm, out_ref, hi, orders_ref, sky, table, raw_a, raw_b, sums, sems
):
    raws = (raw_a, raw_b)
    blocks = sky.shape[1]
    pairs = hi.shape[0]
    count = orders_ref.shape[1]
    map_count = sky.shape[0] // pairs
    inner = BF16_ROWS // HEMIS
    small = [
        pltpu.make_async_copy(orders_hbm, orders_ref, sems.at[0]),
        pltpu.make_async_copy(hi_hbm, hi, sems.at[1]),
    ]
    copies = []
    for c, (start, size) in enumerate(spans):
        part = pl.ds(start * pairs, size * pairs)
        copies.append(pltpu.make_async_copy(sky_hbm.at[part], sky.at[part], sems.at[2 + c]))
    for copy in small + copies:
        copy.start()

    gather = pair_rows(pairs)
    for copy in small:
        copy.wait()
    orders = orders_ref[...]
    cos_l, sin_l = unit_circle(orders * iota((LANES, count), 0) & (NPIX_HI - 1), NPIX_HI)
    stride = inner * LANES
    cos_a, sin_a = unit_circle(
        orders * (stride * iota((blocks, count), 0)) & (NPIX_HI - 1), NPIX_HI
    )
    scale = 1.0 / math.sqrt(NPIX_HI)
    cos_p, sin_p = [], []
    for p in range(pairs):
        offset = (hi[p] - NSIDE_HI + 1) & 1
        step = 2 * LANES * (iota((BF16_ROWS, count), 0) // HEMIS) + offset
        cosine, sine = unit_circle(orders * step & (2 * NPIX_HI - 1), 2 * NPIX_HI)
        cos_p.append(cosine * scale)
        sin_p.append(sine * scale)
    copies[0].wait()
    for a in range(blocks):
        ca, sa = cos_a[a : a + 1], sin_a[a : a + 1]
        table[a * LANES : (a + 1) * LANES, :count] = (ca * cos_l - sa * sin_l).astype(BF16)
        table[a * LANES : (a + 1) * LANES, count:] = (sa * cos_l + ca * sin_l).astype(BF16)

    def contract(c):
        start, size = spans[c]
        part = slice(start * pairs, (start + size) * pairs)
        rows = jnp.concatenate(
            [sky[part, a].reshape(size * pairs * BF16_ROWS, LANES) for a in range(blocks)], axis=1
        )
        full = size * pairs * BF16_ROWS
        raws[c % 2][: full // 2] = dot_nn(rows[: full // 2], table[...])
        raws[c % 2][full // 2 : full] = dot_nn(rows[full // 2 :], table[...])

    sub = iota((1, F32_ROWS, count), 1)

    def sum_blocks(value):
        value = value[:, :F32_ROWS] + value[:, F32_ROWS:]
        low, high = value[:4], value[4:]
        first = sub < 4
        value = jnp.where(first, low, high) + pltpu.roll(jnp.where(first, high, low), 4, 1)
        low, high = value[:2], value[2:]
        first = (sub & 2) == 0
        value = jnp.where(first, low + pltpu.roll(low, 6, 1), high + pltpu.roll(high, 2, 1))
        low, high = value[:1], value[1:]
        first = (sub & 1) == 0
        north = jnp.where(first, low, pltpu.roll(high, 1, 1))
        south = jnp.where(first, pltpu.roll(low, 7, 1), high)
        return north[0], south[0]

    def finish(c):
        start, size = spans[c]
        rows = 8 * pairs * BF16_ROWS
        for group in range(size // 8):
            raw = raws[c % 2][group * rows : (group + 1) * rows]
            raw = raw.reshape(8, pairs, BF16_ROWS, 2 * count)
            at = start + group * 8
            for p in range(pairs):
                raw_c, raw_s = raw[:, p, :, :count], raw[:, p, :, count:]
                cosine, sine = cos_p[p][None], sin_p[p][None]
                real = sum_blocks(raw_c * cosine - raw_s * sine)
                imag = sum_blocks(raw_c * sine + raw_s * cosine)
                for h in range(HEMIS):
                    sums[p, h, 0, at : at + 8] = real[h]
                    sums[p, h, 1, at : at + 8] = -imag[h]

    contract(0)
    for c in range(1, len(spans)):
        copies[c].wait()
        contract(c)
        finish(c - 1)
    finish(len(spans) - 1)
    cols = HEMIS * 2 * map_count
    for j in range(count // LANES):
        lanes = slice(j * LANES, (j + 1) * LANES)
        held = [sums[p, :, :, :, lanes].reshape(cols, LANES).astype(BF16) for p in range(pairs)]
        block = dot_nt(gather, jnp.concatenate(held, axis=1))
        out_ref[j * LANES * pairs : (j + 1) * LANES * pairs] = block.astype(BF16)


def inverse_table_kernel(
    pairs, lo_ref, orders_ref, column_ref, table_ref, residue_ref, gather_ref, phase_ref
):
    count = column_ref.shape[0]
    orders = orders_ref[...]
    scale = math.sqrt(2.0 / count)
    for p in range(pairs):
        offset = (lo_ref[p] - NSIDE_LO + 1) & 1
        step = 2 * LANES * (iota((F32_ROWS, count), 0) // HEMIS) + offset
        cosine, sine = unit_circle(orders * step & (2 * NPIX_LO - 1), 2 * NPIX_LO)
        phase_ref[p, 0] = cosine * scale
        phase_ref[p, 1] = sine * scale
    column = column_ref[...]
    step = F32_ROWS // HEMIS * LANES
    cosine, sine = unit_circle(column * iota((count, LANES), 1) & (NPIX_LO - 1), NPIX_LO)
    cos_step, sin_step = unit_circle(
        jnp.broadcast_to(column * step & (NPIX_LO - 1), (count, LANES)), NPIX_LO
    )
    for a in range(table_ref.shape[1] // LANES):
        lanes = slice(a * LANES, (a + 1) * LANES)
        table_ref[:count, lanes], residue_ref[:count, lanes] = split(cosine)
        table_ref[count:, lanes], residue_ref[count:, lanes] = split(-sine)
        cosine, sine = (
            cosine * cos_step - sine * sin_step,
            sine * cos_step + cosine * sin_step,
        )
    gather_ref[...] = pair_rows(pairs)


def slot_rows(owned, pairs, pair_total):
    shape = (pair_total * owned, owned * pair_total)
    column = iota((1, shape[1]), 1)
    slot, pair = column // pair_total, column % pair_total
    home = (pair // pairs * owned + slot) * pairs + pair % pairs
    return jnp.where(iota(shape, 0) == home, 1.0, 0.0).astype(BF16)


def prepare_kernel(
    pairs, own_ref, beam_ref, hi_hbm, lo_hbm, weight_ref, sign_ref, gather_ref, hi_out, lo_out, sems
):
    copies = [
        pltpu.make_async_copy(hi_hbm, hi_out, sems.at[0]),
        pltpu.make_async_copy(lo_hbm, lo_out, sems.at[1]),
    ]
    for copy in copies:
        copy.start()
    degrees = iota(beam_ref.shape, 1)
    owned = weight_ref.shape[0]
    for g in range(owned):
        order = own_ref[g]
        weight_ref[g] = jnp.where(degrees >= order, beam_ref[...], 0.0)
        sign_ref[g] = (1 - 2 * ((degrees + order) & 1)).astype(F32).astype(BF16)
    gather_ref[...] = slot_rows(owned, pairs, gather_ref.shape[0] // owned)
    for copy in copies:
        copy.wait()


def harmonic_kernel(
    same, low_pairs, received_ref, weight_ref, sign_ref, gather_ref, hi_ref, lo_ref, out_ref, held
):
    owned, pair_total = hi_ref.shape[:2]
    low_total = lo_ref.shape[1]
    half = received_ref.shape[1] // HEMIS
    north = dot_tn(received_ref[:, :half], gather_ref[...])
    south = dot_tn(received_ref[:, half:], gather_ref[...])
    for g in range(owned):
        lanes = slice(g * pair_total, (g + 1) * pair_total)
        coeffs = jnp.concatenate([north[:, lanes], south[:, lanes]], axis=1).astype(BF16)
        hi_table = jnp.concatenate([hi_ref[g], hi_ref[g] * sign_ref[g]], axis=0)
        alm = dot_nn(coeffs, hi_table) * weight_ref[g]
        lo_table = jnp.concatenate([lo_ref[g], lo_ref[g] * sign_ref[g]], axis=0)
        total = dot_nt(lo_table, alm.astype(BF16)).astype(BF16)
        for h in range(HEMIS):
            held[g * low_total : (g + 1) * low_total, h * half : (h + 1) * half] = total[
                h * low_total : (h + 1) * low_total
            ]
    scatter = gather_ref[...] if same else slot_rows(owned, low_pairs, low_total)
    out_ref[...] = dot_nn(scatter, held[...]).astype(BF16)


def synthesise_kernel(
    phase_ref, table_ref, residue_ref, gather_ref, returned_ref, out_hbm,
    spectra, high, low, buffer, sems,
):
    pairs, steps, map_count, wide = buffer.shape[:4]
    count = phase_ref.shape[3]
    for j in range(count // LANES):
        rows = slice(j * LANES * pairs, (j + 1) * LANES * pairs)
        turned = dot_tn(returned_ref[rows], gather_ref[...])
        for p in range(pairs):
            spectra[p, :, j * LANES : (j + 1) * LANES] = turned[:, p * LANES : (p + 1) * LANES]

    south = (iota((F32_ROWS, count), 0) & 1) == 1

    def turn(p, i):
        def spread(c):
            north = spectra[p, c * map_count + i : c * map_count + i + 1]
            at = (2 + c) * map_count + i
            return jnp.where(south, spectra[p, at : at + 1], north)

        real, imag = spread(0), spread(1)
        cosine, sine = phase_ref[p, 0], phase_ref[p, 1]
        return real * cosine - imag * sine, imag * cosine + real * sine

    def rotate(p, first, last):
        for i in range(first, last, 2):
            at = slice((p * map_count + i) * F32_ROWS, (p * map_count + i + 2) * F32_ROWS)
            for c, parts in enumerate(zip(turn(p, i), turn(p, i + 1))):
                lanes = slice(c * count, (c + 1) * count)
                high[at, lanes], low[at, lanes] = split(jnp.concatenate(parts, axis=0))

    copies = []
    rotate(0, 0, map_count)
    for p in range(pairs):
        rows = slice(p * map_count * F32_ROWS, (p + 1) * map_count * F32_ROWS)
        for n in range(steps):
            lanes = slice(n * wide * LANES, (n + 1) * wide * LANES)
            pixels = dot_nn(high[rows], table_ref[:, lanes]) + dot_nn(low[rows], table_ref[:, lanes])
            pixels += dot_nn(high[rows], residue_ref[:, lanes])
            if p + 1 < pairs:
                share = map_count // steps
                rotate(p + 1, n * share, (n + 1) * share)
            pixels = pixels.reshape(map_count, F32_ROWS, wide * LANES)
            for a in range(wide):
                buffer[p, n, :, a] = pixels[:, :, a * LANES : (a + 1) * LANES]
            target = out_hbm.at[:, p, pl.ds(n * wide, wide)]
            copies.append(pltpu.make_async_copy(buffer.at[p, n], target, sems.at[p, n]))
            copies[-1].start()
    for copy in copies:
        copy.wait()


def vmem():
    return pl.BlockSpec(memory_space=pltpu.VMEM)


def smem():
    return pl.BlockSpec(memory_space=pltpu.SMEM)


def hbm():
    return pl.BlockSpec(memory_space=pltpu.HBM)


def params(grant=WHOLE_VMEM):
    return pltpu.CompilerParams(vmem_limit_bytes=grant)


def struct(shape, dtype):
    return jax.ShapeDtypeStruct(shape, dtype)


def analyse(sky_maps, hi_cycles, azimuth_orders):
    map_count, pairs = sky_maps.shape[:2]
    count = azimuth_orders.shape[0]
    cols = HEMIS * 2 * map_count
    inner = BF16_ROWS // HEMIS
    blocks = NPIX_HI // (inner * LANES)
    sky = sky_maps.reshape(map_count, pairs, HEMIS, blocks, inner, LANES)
    sky = sky.transpose(0, 1, 3, 4, 2, 5)
    sky = sky.reshape(map_count * pairs, blocks, BF16_ROWS, LANES)
    size = map_count // 4
    spans = [(k * size, size) for k in range(4)]
    raw = pltpu.VMEM((size * pairs * BF16_ROWS, 2 * count), F32)
    return pl.pallas_call(
        functools.partial(analyse_kernel, spans),
        out_shape=struct((count * pairs, cols), BF16),
        in_specs=[hbm(), hbm(), hbm()],
        out_specs=vmem(),
        scratch_shapes=[
            pltpu.SMEM((pairs,), jnp.int32),
            pltpu.VMEM((1, count), jnp.int32),
            pltpu.VMEM((map_count * pairs, blocks, BF16_ROWS, LANES), BF16),
            pltpu.VMEM((blocks * LANES, 2 * count), BF16),
            raw,
            raw,
            pltpu.VMEM((pairs, HEMIS, 2, map_count, count), F32),
            pltpu.SemaphoreType.DMA((2 + len(spans),)),
        ],
        compiler_params=params(),
        name="analyse",
    )(hi_cycles, azimuth_orders.reshape(1, count), sky)


def per_device(
    sky_maps, hi_cycles, lo_cycles, azimuth_orders, legendre_hi, legendre_lo, beam_weights
):
    axes = ("band", "ma")
    map_count, pairs = sky_maps.shape[:2]
    low_pairs = lo_cycles.shape[0]
    count = azimuth_orders.shape[0]
    owned, degree_count, pair_total = legendre_hi.shape
    low_total = legendre_lo.shape[2]
    devices = count // owned
    order_row = azimuth_orders.reshape(1, count)
    order_column = azimuth_orders.reshape(count, 1)
    cols = HEMIS * 2 * map_count

    outgoing = analyse(sky_maps, hi_cycles, azimuth_orders)
    received = lax.all_to_all(
        outgoing.reshape(devices, owned * pairs, cols), axes, split_axis=0, concat_axis=0, tiled=True
    )

    rows = count * pairs
    own = lax.dynamic_slice_in_dim(azimuth_orders, lax.axis_index(axes) * owned, owned)
    low_rows = count * low_pairs
    same = (low_pairs, low_total) == (pairs, pair_total)
    hi_blocks, lo_blocks = legendre_hi.transpose(0, 2, 1), legendre_lo.transpose(0, 2, 1)
    prepared = pl.pallas_call(
        functools.partial(prepare_kernel, pairs),
        out_shape=[
            struct((owned, 1, degree_count), F32),
            struct((owned, 1, degree_count), BF16),
            struct((rows, owned * pair_total), BF16),
            struct(hi_blocks.shape, BF16),
            struct(lo_blocks.shape, BF16),
        ],
        in_specs=[smem(), vmem(), hbm(), hbm()],
        out_specs=[vmem()] * 5,
        scratch_shapes=[pltpu.SemaphoreType.DMA((2,))],
        compiler_params=params(50 * 2**20),
        cost_estimate=pl.CostEstimate(
            flops=2**10 * degree_count, bytes_accessed=2**10 * degree_count, transcendentals=0
        ),
        name="prepare",
    )(own, beam_weights.reshape(1, degree_count), hi_blocks, lo_blocks)
    synthesised = pl.pallas_call(
        functools.partial(harmonic_kernel, same, low_pairs),
        out_shape=struct((low_rows, cols), BF16),
        in_specs=[vmem()] * 6,
        out_specs=vmem(),
        scratch_shapes=[pltpu.VMEM((owned * low_total, cols), BF16)],
        compiler_params=params(16 * 2**20),
        name="harmonic",
    )(received.reshape(rows, cols), *prepared)
    returned = lax.all_to_all(
        synthesised.reshape(devices, owned * low_pairs, cols),
        axes,
        split_axis=0,
        concat_axis=0,
        tiled=True,
    )

    blocks_lo = NPIX_LO // (F32_ROWS // HEMIS * LANES)
    side = LANES * low_pairs
    inverse_table, residue, regroup, phase = pl.pallas_call(
        functools.partial(inverse_table_kernel, low_pairs),
        out_shape=[
            struct((2 * count, blocks_lo * LANES), BF16),
            struct((2 * count, blocks_lo * LANES), BF16),
            struct((side, side), BF16),
            struct((low_pairs, 2, F32_ROWS, count), F32),
        ],
        in_specs=[smem(), vmem(), vmem()],
        out_specs=[vmem()] * 4,
        compiler_params=params(8 * 2**20),
        cost_estimate=pl.CostEstimate(
            flops=64 * count * blocks_lo * LANES,
            bytes_accessed=8 * count * blocks_lo * LANES,
            transcendentals=0,
        ),
        name="inverse_table",
    )(lo_cycles, order_row, order_column)
    steps = 2
    wide = blocks_lo // steps
    buffer = pltpu.VMEM((low_pairs, steps, map_count, wide, F32_ROWS, LANES), F32)
    spectrum = pltpu.VMEM((map_count * low_pairs * F32_ROWS, 2 * count), BF16)
    pixels = pl.pallas_call(
        synthesise_kernel,
        out_shape=struct((map_count, low_pairs, blocks_lo, F32_ROWS, LANES), F32),
        in_specs=[vmem()] * 5,
        out_specs=hbm(),
        scratch_shapes=[
            pltpu.VMEM((low_pairs, cols, count), F32),
            spectrum,
            spectrum,
            buffer,
            pltpu.SemaphoreType.DMA((low_pairs, steps)),
        ],
        compiler_params=params(32 * 2**20),
        name="synthesise",
    )(phase, inverse_table, residue, regroup, returned.reshape(low_rows, cols))
    pixels = pixels.reshape(map_count, low_pairs, blocks_lo, F32_ROWS // HEMIS, HEMIS, LANES)
    pixels = pixels.transpose(0, 1, 4, 2, 3, 5)
    return pixels.reshape(map_count, low_pairs, HEMIS, NPIX_LO)


def solution(mesh):
    spread = ("band", "ma")
    return jax.shard_map(
        per_device,
        mesh=mesh,
        in_specs=(
            P(None, spread, None, None),
            P(spread),
            P(spread),
            P(),
            P(spread, None, None),
            P(spread, None, None),
            P(),
        ),
        out_specs=P(None, spread, None, None),
        check_vma=False,
    )
```

```python
import functools
import math

import jax
import jax.numpy as jnp
from jax import lax
from jax.experimental import pallas as pl
from jax.experimental.pallas import tpu as pltpu
from jax.sharding import PartitionSpec as P

NSIDE_HI = 4096
NSIDE_LO = 1024
NPIX_HI = 16384
NPIX_LO = 4096

LANES = 128
HEMIS = 2
BF16_ROWS = 16
WHOLE_VMEM = 67_043_328
F32_ROWS = 8
F32 = jnp.float32
BF16 = jnp.bfloat16


def unit_circle(steps, length):
    quarter = length // 4
    quadrant = (steps + quarter // 2) // quarter
    rest = steps - quadrant * quarter
    angle = rest.astype(F32) * (2.0 * math.pi / length)
    square = angle * angle
    sine = square * (1.0 / 362880.0) - 1.0 / 5040.0
    sine = square * sine + 1.0 / 120.0
    sine = square * sine - 1.0 / 6.0
    sine = angle + angle * (square * sine)
    cosine = square * (-1.0 / 3628800.0) + 1.0 / 40320.0
    cosine = square * cosine - 1.0 / 720.0
    cosine = square * cosine + 1.0 / 24.0
    cosine = square * cosine - 0.5
    cosine = 1.0 + square * cosine
    odd = (quadrant & 1) == 1
    big = jnp.where(odd, sine, cosine)
    small = jnp.where(odd, cosine, sine)
    cos_out = jnp.where(((quadrant + 1) & 2) == 2, -big, big)
    sin_out = jnp.where((quadrant & 2) == 2, -small, small)
    return cos_out, sin_out


def iota(shape, dim):
    return lax.broadcasted_iota(jnp.int32, shape, dim)


def split(value):
    high = value.astype(BF16)
    return high, (value - high.astype(F32)).astype(BF16)


def one_hot(shape, match):
    return jnp.where(match(iota(shape, 0), iota(shape, 1)), 1.0, 0.0).astype(BF16)


def dot_tn(lhs, rhs):
    return lax.dot_general(lhs, rhs, (((0,), (0,)), ((), ())), preferred_element_type=F32)


def dot_nt(lhs, rhs):
    return lax.dot_general(lhs, rhs, (((1,), (1,)), ((), ())), preferred_element_type=F32)


def dot_nn(lhs, rhs):
    return jnp.dot(lhs, rhs, preferred_element_type=F32)


def pair_rows(pairs):
    side = LANES * pairs
    return one_hot((side, side), lambda i, j: i == j % LANES * pairs + j // LANES)


def analyse_kernel(
    spans, hi_hbm, orders_hbm, sky_hbm, out_ref, hi, orders_ref, sky, table, raw_a, raw_b, sums, sems
):
    raws = (raw_a, raw_b)
    blocks = sky.shape[1]
    pairs = hi.shape[0]
    count = orders_ref.shape[1]
    map_count = sky.shape[0] // pairs
    inner = BF16_ROWS // HEMIS
    small = [
        pltpu.make_async_copy(orders_hbm, orders_ref, sems.at[0]),
        pltpu.make_async_copy(hi_hbm, hi, sems.at[1]),
    ]
    copies = []
    for c, (_, start, size, first, last) in enumerate(spans):
        part = (pl.ds(start * pairs, size * pairs), pl.ds(first, last - first))
        copies.append(pltpu.make_async_copy(sky_hbm.at[part], sky.at[part], sems.at[2 + c]))
    for copy in small + copies:
        copy.start()

    gather = pair_rows(pairs)
    for copy in small:
        copy.wait()
    orders = orders_ref[...]
    cos_l, sin_l = unit_circle(orders * iota((LANES, count), 0) & (NPIX_HI - 1), NPIX_HI)
    stride = inner * LANES
    cos_a, sin_a = unit_circle(
        orders * (stride * iota((blocks, count), 0)) & (NPIX_HI - 1), NPIX_HI
    )
    scale = 1.0 / math.sqrt(NPIX_HI)
    cos_p, sin_p = [], []
    for p in range(pairs):
        offset = (hi[p] - NSIDE_HI + 1) & 1
        step = 2 * LANES * (iota((BF16_ROWS, count), 0) // HEMIS) + offset
        cosine, sine = unit_circle(orders * step & (2 * NPIX_HI - 1), 2 * NPIX_HI)
        cos_p.append(cosine * scale)
        sin_p.append(sine * scale)
    for a in range(blocks):
        ca, sa = cos_a[a : a + 1], sin_a[a : a + 1]
        table[a * LANES : (a + 1) * LANES, :count] = (ca * cos_l - sa * sin_l).astype(BF16)
        table[a * LANES : (a + 1) * LANES, count:] = (sa * cos_l + ca * sin_l).astype(BF16)

    def contract(c):
        chunk, start, size, first, last = spans[c]
        part = slice(start * pairs, (start + size) * pairs)
        full = size * pairs * BF16_ROWS
        rows = jnp.concatenate(
            [sky[part, a].reshape(full, LANES) for a in range(first, last)], axis=1
        )
        depth = slice(first * LANES, last * LANES)
        for half in (slice(0, full // 2), slice(full // 2, full)):
            raw = dot_nn(rows[half], table[depth])
            raws[chunk % 2][half] = raw if first == 0 else raws[chunk % 2][half] + raw

    sub = iota((1, F32_ROWS, count), 1)

    def sum_blocks(value):
        value = value[:, :F32_ROWS] + value[:, F32_ROWS:]
        low, high = value[:4], value[4:]
        first = sub < 4
        value = jnp.where(first, low, high) + pltpu.roll(jnp.where(first, high, low), 4, 1)
        low, high = value[:2], value[2:]
        first = (sub & 2) == 0
        value = jnp.where(first, low + pltpu.roll(low, 6, 1), high + pltpu.roll(high, 2, 1))
        low, high = value[:1], value[1:]
        first = (sub & 1) == 0
        north = jnp.where(first, low, pltpu.roll(high, 1, 1))
        south = jnp.where(first, pltpu.roll(low, 7, 1), high)
        return north[0], south[0]

    def finish(c):
        chunk, start, size, _, last = spans[c]
        if last < blocks:
            return
        rows = 8 * pairs * BF16_ROWS
        for group in range(size // 8):
            raw = raws[chunk % 2][group * rows : (group + 1) * rows]
            raw = raw.reshape(8, pairs, BF16_ROWS, 2 * count)
            at = start + group * 8
            for p in range(pairs):
                raw_c, raw_s = raw[:, p, :, :count], raw[:, p, :, count:]
                cosine, sine = cos_p[p][None], sin_p[p][None]
                real = sum_blocks(raw_c * cosine - raw_s * sine)
                imag = sum_blocks(raw_c * sine + raw_s * cosine)
                for h in range(HEMIS):
                    sums[p, h, 0, at : at + 8] = real[h]
                    sums[p, h, 1, at : at + 8] = -imag[h]

    copies[0].wait()
    contract(0)
    for c in range(1, len(spans)):
        copies[c].wait()
        contract(c)
        finish(c - 1)
    finish(len(spans) - 1)
    cols = HEMIS * 2 * map_count
    for j in range(count // LANES):
        lanes = slice(j * LANES, (j + 1) * LANES)
        held = [sums[p, :, :, :, lanes].reshape(cols, LANES).astype(BF16) for p in range(pairs)]
        block = dot_nt(gather, jnp.concatenate(held, axis=1))
        out_ref[j * LANES * pairs : (j + 1) * LANES * pairs] = block.astype(BF16)


def inverse_table_kernel(
    pairs, lo_ref, orders_ref, column_ref, table_ref, residue_ref, gather_ref, phase_ref
):
    count = column_ref.shape[0]
    orders = orders_ref[...]
    scale = math.sqrt(2.0 / count)
    for p in range(pairs):
        offset = (lo_ref[p] - NSIDE_LO + 1) & 1
        step = 2 * LANES * (iota((F32_ROWS, count), 0) // HEMIS) + offset
        cosine, sine = unit_circle(orders * step & (2 * NPIX_LO - 1), 2 * NPIX_LO)
        phase_ref[p, 0] = cosine * scale
        phase_ref[p, 1] = sine * scale
    column = column_ref[...]
    step = F32_ROWS // HEMIS * LANES
    cosine, sine = unit_circle(column * iota((count, LANES), 1) & (NPIX_LO - 1), NPIX_LO)
    cos_step, sin_step = unit_circle(
        jnp.broadcast_to(column * step & (NPIX_LO - 1), (count, LANES)), NPIX_LO
    )
    for a in range(table_ref.shape[1] // LANES):
        lanes = slice(a * LANES, (a + 1) * LANES)
        table_ref[:count, lanes], residue_ref[:count, lanes] = split(cosine)
        table_ref[count:, lanes], residue_ref[count:, lanes] = split(-sine)
        cosine, sine = (
            cosine * cos_step - sine * sin_step,
            sine * cos_step + cosine * sin_step,
        )
    gather_ref[...] = pair_rows(pairs)


def slot_rows(owned, pairs, pair_total):
    shape = (pair_total * owned, owned * pair_total)
    column = iota((1, shape[1]), 1)
    slot, pair = column // pair_total, column % pair_total
    home = (pair // pairs * owned + slot) * pairs + pair % pairs
    return jnp.where(iota(shape, 0) == home, 1.0, 0.0).astype(BF16)


def prepare_kernel(
    pairs, own_ref, beam_ref, hi_hbm, lo_hbm, weight_ref, sign_ref, gather_ref, hi_out, lo_out, sems
):
    copies = [
        pltpu.make_async_copy(hi_hbm, hi_out, sems.at[0]),
        pltpu.make_async_copy(lo_hbm, lo_out, sems.at[1]),
    ]
    for copy in copies:
        copy.start()
    degrees = iota(beam_ref.shape, 1)
    owned = weight_ref.shape[0]
    for g in range(owned):
        order = own_ref[g]
        weight_ref[g] = jnp.where(degrees >= order, beam_ref[...], 0.0)
        sign_ref[g] = (1 - 2 * ((degrees + order) & 1)).astype(F32).astype(BF16)
    gather_ref[...] = slot_rows(owned, pairs, gather_ref.shape[0] // owned)
    for copy in copies:
        copy.wait()


def harmonic_kernel(
    same, low_pairs, received_ref, weight_ref, sign_ref, gather_ref, hi_ref, lo_ref, out_ref, held
):
    owned, pair_total = hi_ref.shape[:2]
    low_total = lo_ref.shape[1]
    half = received_ref.shape[1] // HEMIS
    north = dot_tn(received_ref[:, :half], gather_ref[...])
    south = dot_tn(received_ref[:, half:], gather_ref[...])
    def analyse_slot(g):
        lanes = slice(g * pair_total, (g + 1) * pair_total)
        coeffs = jnp.concatenate([north[:, lanes], south[:, lanes]], axis=1).astype(BF16)
        hi_table = jnp.concatenate([hi_ref[g], hi_ref[g] * sign_ref[g]], axis=0)
        return (dot_nn(coeffs, hi_table) * weight_ref[g]).astype(BF16)

    alms = [analyse_slot(g) for g in range(1)]
    for g in range(owned):
        if g + 1 < owned:
            alms.append(analyse_slot(g + 1))
        lo_table = jnp.concatenate([lo_ref[g], lo_ref[g] * sign_ref[g]], axis=0)
        total = dot_nt(lo_table, alms[g]).astype(BF16)
        for h in range(HEMIS):
            held[g * low_total : (g + 1) * low_total, h * half : (h + 1) * half] = total[
                h * low_total : (h + 1) * low_total
            ]
    scatter = gather_ref[...] if same else slot_rows(owned, low_pairs, low_total)
    out_ref[...] = dot_nn(scatter, held[...]).astype(BF16)


def synthesise_kernel(
    phase_ref, table_ref, residue_ref, gather_ref, returned_ref, out_hbm,
    spectra, high, low, buffer, sems,
):
    pairs, steps, map_count, wide = buffer.shape[:4]
    count = phase_ref.shape[3]
    for j in range(count // LANES):
        rows = slice(j * LANES * pairs, (j + 1) * LANES * pairs)
        turned = dot_tn(returned_ref[rows], gather_ref[...])
        for p in range(pairs):
            spectra[p, :, j * LANES : (j + 1) * LANES] = turned[:, p * LANES : (p + 1) * LANES]

    south = (iota((F32_ROWS, count), 0) & 1) == 1

    def turn(p, i):
        def spread(c):
            north = spectra[p, c * map_count + i : c * map_count + i + 1]
            at = (2 + c) * map_count + i
            return jnp.where(south, spectra[p, at : at + 1], north)

        real, imag = spread(0), spread(1)
        cosine, sine = phase_ref[p, 0], phase_ref[p, 1]
        return real * cosine - imag * sine, imag * cosine + real * sine

    def rotate(p, first, last):
        for i in range(first, last, 2):
            at = slice((p * map_count + i) * F32_ROWS, (p * map_count + i + 2) * F32_ROWS)
            for c, parts in enumerate(zip(turn(p, i), turn(p, i + 1))):
                lanes = slice(c * count, (c + 1) * count)
                high[at, lanes], low[at, lanes] = split(jnp.concatenate(parts, axis=0))

    copies = []
    rotate(0, 0, map_count)
    for p in range(pairs):
        rows = slice(p * map_count * F32_ROWS, (p + 1) * map_count * F32_ROWS)
        for n in range(steps):
            lanes = slice(n * wide * LANES, (n + 1) * wide * LANES)
            pixels = dot_nn(high[rows], table_ref[:, lanes]) + dot_nn(low[rows], table_ref[:, lanes])
            pixels += dot_nn(high[rows], residue_ref[:, lanes])
            if p + 1 < pairs:
                share = map_count // steps
                rotate(p + 1, n * share, (n + 1) * share)
            pixels = pixels.reshape(map_count, F32_ROWS, wide * LANES)
            for a in range(wide):
                buffer[p, n, :, a] = pixels[:, :, a * LANES : (a + 1) * LANES]
            target = out_hbm.at[:, p, pl.ds(n * wide, wide)]
            copies.append(pltpu.make_async_copy(buffer.at[p, n], target, sems.at[p, n]))
            copies[-1].start()
    for copy in copies:
        copy.wait()


def vmem():
    return pl.BlockSpec(memory_space=pltpu.VMEM)


def smem():
    return pl.BlockSpec(memory_space=pltpu.SMEM)


def hbm():
    return pl.BlockSpec(memory_space=pltpu.HBM)


def params(grant=WHOLE_VMEM):
    return pltpu.CompilerParams(vmem_limit_bytes=grant)


def struct(shape, dtype):
    return jax.ShapeDtypeStruct(shape, dtype)


def analyse(sky_maps, hi_cycles, azimuth_orders):
    map_count, pairs = sky_maps.shape[:2]
    count = azimuth_orders.shape[0]
    cols = HEMIS * 2 * map_count
    inner = BF16_ROWS // HEMIS
    blocks = NPIX_HI // (inner * LANES)
    sky = sky_maps.reshape(map_count, pairs, HEMIS, blocks, inner, LANES)
    sky = sky.transpose(0, 1, 3, 4, 2, 5)
    sky = sky.reshape(map_count * pairs, blocks, BF16_ROWS, LANES)
    size = map_count // 4
    spans = []
    for k in range(4):
        edges = (0, blocks // 2, blocks) if k in (0, 3) else (0, blocks)
        spans += [(k, k * size, size, *edge) for edge in zip(edges, edges[1:])]
    raw = pltpu.VMEM((size * pairs * BF16_ROWS, 2 * count), F32)
    return pl.pallas_call(
        functools.partial(analyse_kernel, spans),
        out_shape=struct((count * pairs, cols), BF16),
        in_specs=[hbm(), hbm(), hbm()],
        out_specs=vmem(),
        scratch_shapes=[
            pltpu.SMEM((pairs,), jnp.int32),
            pltpu.VMEM((1, count), jnp.int32),
            pltpu.VMEM((map_count * pairs, blocks, BF16_ROWS, LANES), BF16),
            pltpu.VMEM((blocks * LANES, 2 * count), BF16),
            raw,
            raw,
            pltpu.VMEM((pairs, HEMIS, 2, map_count, count), F32),
            pltpu.SemaphoreType.DMA((2 + len(spans),)),
        ],
        compiler_params=params(),
        name="analyse",
    )(hi_cycles, azimuth_orders.reshape(1, count), sky)


def per_device(
    sky_maps, hi_cycles, lo_cycles, azimuth_orders, legendre_hi, legendre_lo, beam_weights
):
    axes = ("band", "ma")
    map_count, pairs = sky_maps.shape[:2]
    low_pairs = lo_cycles.shape[0]
    count = azimuth_orders.shape[0]
    owned, degree_count, pair_total = legendre_hi.shape
    low_total = legendre_lo.shape[2]
    devices = count // owned
    order_row = azimuth_orders.reshape(1, count)
    order_column = azimuth_orders.reshape(count, 1)
    cols = HEMIS * 2 * map_count

    outgoing = analyse(sky_maps, hi_cycles, azimuth_orders)
    received = lax.all_to_all(
        outgoing.reshape(devices, owned * pairs, cols), axes, split_axis=0, concat_axis=0, tiled=True
    )

    rows = count * pairs
    own = lax.dynamic_slice_in_dim(azimuth_orders, lax.axis_index(axes) * owned, owned)
    low_rows = count * low_pairs
    same = (low_pairs, low_total) == (pairs, pair_total)
    hi_blocks, lo_blocks = legendre_hi.transpose(0, 2, 1), legendre_lo.transpose(0, 2, 1)
    prepared = pl.pallas_call(
        functools.partial(prepare_kernel, pairs),
        out_shape=[
            struct((owned, 1, degree_count), F32),
            struct((owned, 1, degree_count), BF16),
            struct((rows, owned * pair_total), BF16),
            struct(hi_blocks.shape, BF16),
            struct(lo_blocks.shape, BF16),
        ],
        in_specs=[smem(), vmem(), hbm(), hbm()],
        out_specs=[vmem()] * 5,
        scratch_shapes=[pltpu.SemaphoreType.DMA((2,))],
        compiler_params=params(50 * 2**20),
        cost_estimate=pl.CostEstimate(
            flops=2**10 * degree_count, bytes_accessed=2**10 * degree_count, transcendentals=0
        ),
        name="prepare",
    )(own, beam_weights.reshape(1, degree_count), hi_blocks, lo_blocks)
    synthesised = pl.pallas_call(
        functools.partial(harmonic_kernel, same, low_pairs),
        out_shape=struct((low_rows, cols), BF16),
        in_specs=[vmem()] * 6,
        out_specs=vmem(),
        scratch_shapes=[pltpu.VMEM((owned * low_total, cols), BF16)],
        compiler_params=params(16 * 2**20),
        name="harmonic",
    )(received.reshape(rows, cols), *prepared)
    returned = lax.all_to_all(
        synthesised.reshape(devices, owned * low_pairs, cols),
        axes,
        split_axis=0,
        concat_axis=0,
        tiled=True,
    )

    blocks_lo = NPIX_LO // (F32_ROWS // HEMIS * LANES)
    side = LANES * low_pairs
    inverse_table, residue, regroup, phase = pl.pallas_call(
        functools.partial(inverse_table_kernel, low_pairs),
        out_shape=[
            struct((2 * count, blocks_lo * LANES), BF16),
            struct((2 * count, blocks_lo * LANES), BF16),
            struct((side, side), BF16),
            struct((low_pairs, 2, F32_ROWS, count), F32),
        ],
        in_specs=[smem(), vmem(), vmem()],
        out_specs=[vmem()] * 4,
        compiler_params=params(8 * 2**20),
        cost_estimate=pl.CostEstimate(
            flops=64 * count * blocks_lo * LANES,
            bytes_accessed=8 * count * blocks_lo * LANES,
            transcendentals=0,
        ),
        name="inverse_table",
    )(lo_cycles, order_row, order_column)
    steps = 2
    wide = blocks_lo // steps
    buffer = pltpu.VMEM((low_pairs, steps, map_count, wide, F32_ROWS, LANES), F32)
    spectrum = pltpu.VMEM((map_count * low_pairs * F32_ROWS, 2 * count), BF16)
    pixels = pl.pallas_call(
        synthesise_kernel,
        out_shape=struct((map_count, low_pairs, blocks_lo, F32_ROWS, LANES), F32),
        in_specs=[vmem()] * 5,
        out_specs=hbm(),
        scratch_shapes=[
            pltpu.VMEM((low_pairs, cols, count), F32),
            spectrum,
            spectrum,
            buffer,
            pltpu.SemaphoreType.DMA((low_pairs, steps)),
        ],
        compiler_params=params(32 * 2**20),
        name="synthesise",
    )(phase, inverse_table, residue, regroup, returned.reshape(low_rows, cols))
    pixels = pixels.reshape(map_count, low_pairs, blocks_lo, F32_ROWS // HEMIS, HEMIS, LANES)
    pixels = pixels.transpose(0, 1, 4, 2, 3, 5)
    return pixels.reshape(map_count, low_pairs, HEMIS, NPIX_LO)


def solution(mesh):
    spread = ("band", "ma")
    return jax.shard_map(
        per_device,
        mesh=mesh,
        in_specs=(
            P(None, spread, None, None),
            P(spread),
            P(spread),
            P(),
            P(spread, None, None),
            P(spread, None, None),
            P(),
        ),
        out_specs=P(None, spread, None, None),
        check_vma=False,
    )
```

```python
import functools
import math

import jax
import jax.numpy as jnp
from jax import lax
from jax.experimental import pallas as pl
from jax.experimental.pallas import tpu as pltpu
from jax.sharding import PartitionSpec as P

NSIDE_HI = 4096
NSIDE_LO = 1024
NPIX_HI = 16384
NPIX_LO = 4096

LANES = 128
HEMIS = 2
BF16_ROWS = 16
WHOLE_VMEM = 67_043_328
F32_ROWS = 8
F32 = jnp.float32
BF16 = jnp.bfloat16


def unit_circle(steps, length):
    quarter = length // 4
    quadrant = (steps + quarter // 2) // quarter
    rest = steps - quadrant * quarter
    angle = rest.astype(F32) * (2.0 * math.pi / length)
    square = angle * angle
    sine = square * (1.0 / 362880.0) - 1.0 / 5040.0
    sine = square * sine + 1.0 / 120.0
    sine = square * sine - 1.0 / 6.0
    sine = angle + angle * (square * sine)
    cosine = square * (-1.0 / 3628800.0) + 1.0 / 40320.0
    cosine = square * cosine - 1.0 / 720.0
    cosine = square * cosine + 1.0 / 24.0
    cosine = square * cosine - 0.5
    cosine = 1.0 + square * cosine
    odd = (quadrant & 1) == 1
    big = jnp.where(odd, sine, cosine)
    small = jnp.where(odd, cosine, sine)
    cos_out = jnp.where(((quadrant + 1) & 2) == 2, -big, big)
    sin_out = jnp.where((quadrant & 2) == 2, -small, small)
    return cos_out, sin_out


def iota(shape, dim):
    return lax.broadcasted_iota(jnp.int32, shape, dim)


def split(value):
    high = value.astype(BF16)
    return high, (value - high.astype(F32)).astype(BF16)


def one_hot(shape, match):
    return jnp.where(match(iota(shape, 0), iota(shape, 1)), 1.0, 0.0).astype(BF16)


def dot_tn(lhs, rhs):
    return lax.dot_general(lhs, rhs, (((0,), (0,)), ((), ())), preferred_element_type=F32)


def dot_nt(lhs, rhs):
    return lax.dot_general(lhs, rhs, (((1,), (1,)), ((), ())), preferred_element_type=F32)


def dot_nn(lhs, rhs):
    return jnp.dot(lhs, rhs, preferred_element_type=F32)


def pair_rows(pairs):
    side = LANES * pairs
    return one_hot((side, side), lambda i, j: i == j % LANES * pairs + j // LANES)


def analyse_kernel(
    spans, hi_hbm, orders_hbm, sky_hbm, out_ref, hi, orders_ref, sky, table, raw_a, raw_b, sums, sems
):
    raws = (raw_a, raw_b)
    blocks = sky.shape[1]
    pairs = hi.shape[0]
    count = orders_ref.shape[1]
    map_count = sky.shape[0] // pairs
    inner = BF16_ROWS // HEMIS
    small = [
        pltpu.make_async_copy(orders_hbm, orders_ref, sems.at[0]),
        pltpu.make_async_copy(hi_hbm, hi, sems.at[1]),
    ]
    copies = []
    for c, (_, start, size, first, last) in enumerate(spans):
        part = (pl.ds(start * pairs, size * pairs), pl.ds(first, last - first))
        copies.append(pltpu.make_async_copy(sky_hbm.at[part], sky.at[part], sems.at[2 + c]))
    for copy in small + copies:
        copy.start()

    gather = pair_rows(pairs)
    for copy in small:
        copy.wait()
    orders = orders_ref[...]
    cos_l, sin_l = unit_circle(orders * iota((LANES, count), 0) & (NPIX_HI - 1), NPIX_HI)
    stride = inner * LANES
    cos_a, sin_a = unit_circle(
        orders * (stride * iota((blocks, count), 0)) & (NPIX_HI - 1), NPIX_HI
    )
    scale = 1.0 / math.sqrt(NPIX_HI)
    cos_p, sin_p = [], []
    for p in range(pairs):
        offset = (hi[p] - NSIDE_HI + 1) & 1
        step = 2 * LANES * (iota((BF16_ROWS, count), 0) // HEMIS) + offset
        cosine, sine = unit_circle(orders * step & (2 * NPIX_HI - 1), 2 * NPIX_HI)
        cos_p.append(cosine * scale)
        sin_p.append(sine * scale)
    for a in range(blocks):
        ca, sa = cos_a[a : a + 1], sin_a[a : a + 1]
        table[a * LANES : (a + 1) * LANES, :count] = (ca * cos_l - sa * sin_l).astype(BF16)
        table[a * LANES : (a + 1) * LANES, count:] = (sa * cos_l + ca * sin_l).astype(BF16)

    def contract(c):
        chunk, start, size, first, last = spans[c]
        part = slice(start * pairs, (start + size) * pairs)
        full = size * pairs * BF16_ROWS
        rows = jnp.concatenate(
            [sky[part, a].reshape(full, LANES) for a in range(first, last)], axis=1
        )
        depth = slice(first * LANES, last * LANES)
        for half in (slice(0, full // 2), slice(full // 2, full)):
            raw = dot_nn(rows[half], table[depth])
            raws[chunk % 2][half] = raw if first == 0 else raws[chunk % 2][half] + raw

    sub = iota((1, F32_ROWS, count), 1)

    def sum_blocks(value):
        value = value[:, :F32_ROWS] + value[:, F32_ROWS:]
        low, high = value[:4], value[4:]
        first = sub < 4
        value = jnp.where(first, low, high) + pltpu.roll(jnp.where(first, high, low), 4, 1)
        low, high = value[:2], value[2:]
        first = (sub & 2) == 0
        value = jnp.where(first, low + pltpu.roll(low, 6, 1), high + pltpu.roll(high, 2, 1))
        low, high = value[:1], value[1:]
        first = (sub & 1) == 0
        north = jnp.where(first, low, pltpu.roll(high, 1, 1))
        south = jnp.where(first, pltpu.roll(low, 7, 1), high)
        return north[0], south[0]

    def finish(c):
        chunk, start, size, _, last = spans[c]
        if last < blocks:
            return
        rows = 8 * pairs * BF16_ROWS
        for group in range(size // 8):
            raw = raws[chunk % 2][group * rows : (group + 1) * rows]
            raw = raw.reshape(8, pairs, BF16_ROWS, 2 * count)
            at = start + group * 8
            for p in range(pairs):
                raw_c, raw_s = raw[:, p, :, :count], raw[:, p, :, count:]
                cosine, sine = cos_p[p][None], sin_p[p][None]
                real = sum_blocks(raw_c * cosine - raw_s * sine)
                imag = sum_blocks(raw_c * sine + raw_s * cosine)
                for h in range(HEMIS):
                    sums[p, h, 0, at : at + 8] = real[h]
                    sums[p, h, 1, at : at + 8] = -imag[h]

    copies[0].wait()
    contract(0)
    for c in range(1, len(spans)):
        copies[c].wait()
        contract(c)
        finish(c - 1)
    finish(len(spans) - 1)
    cols = HEMIS * 2 * map_count
    for j in range(count // LANES):
        lanes = slice(j * LANES, (j + 1) * LANES)
        held = [sums[p, :, :, :, lanes].reshape(cols, LANES).astype(BF16) for p in range(pairs)]
        block = dot_nt(gather, jnp.concatenate(held, axis=1))
        out_ref[j * LANES * pairs : (j + 1) * LANES * pairs] = block.astype(BF16)


def inverse_table_kernel(
    pairs, lo_ref, orders_ref, column_ref, table_ref, residue_ref, gather_ref, phase_ref
):
    count = column_ref.shape[0]
    orders = orders_ref[...]
    scale = math.sqrt(2.0 / count)
    for p in range(pairs):
        offset = (lo_ref[p] - NSIDE_LO + 1) & 1
        step = 2 * LANES * (iota((F32_ROWS, count), 0) // HEMIS) + offset
        cosine, sine = unit_circle(orders * step & (2 * NPIX_LO - 1), 2 * NPIX_LO)
        phase_ref[p, 0] = cosine * scale
        phase_ref[p, 1] = sine * scale
    column = column_ref[...]
    step = F32_ROWS // HEMIS * LANES
    cosine, sine = unit_circle(column * iota((count, LANES), 1) & (NPIX_LO - 1), NPIX_LO)
    cos_step, sin_step = unit_circle(
        jnp.broadcast_to(column * step & (NPIX_LO - 1), (count, LANES)), NPIX_LO
    )
    for a in range(table_ref.shape[1] // LANES):
        lanes = slice(a * LANES, (a + 1) * LANES)
        table_ref[:count, lanes], residue_ref[:count, lanes] = split(cosine)
        table_ref[count:, lanes], residue_ref[count:, lanes] = split(-sine)
        cosine, sine = (
            cosine * cos_step - sine * sin_step,
            sine * cos_step + cosine * sin_step,
        )
    gather_ref[...] = pair_rows(pairs)


def slot_rows(owned, pairs, pair_total):
    shape = (pair_total * owned, owned * pair_total)
    column = iota((1, shape[1]), 1)
    slot, pair = column // pair_total, column % pair_total
    home = (pair // pairs * owned + slot) * pairs + pair % pairs
    return jnp.where(iota(shape, 0) == home, 1.0, 0.0).astype(BF16)


def prepare_kernel(
    pairs, own_ref, beam_ref, hi_hbm, lo_hbm, weight_ref, sign_ref, gather_ref, hi_out, lo_out, sems
):
    copies = [
        pltpu.make_async_copy(hi_hbm, hi_out, sems.at[0]),
        pltpu.make_async_copy(lo_hbm, lo_out, sems.at[1]),
    ]
    for copy in copies:
        copy.start()
    degrees = iota(beam_ref.shape, 1)
    owned = weight_ref.shape[0]
    for g in range(owned):
        order = own_ref[g]
        weight_ref[g] = jnp.where(degrees >= order, beam_ref[...], 0.0)
        sign_ref[g] = (1 - 2 * ((degrees + order) & 1)).astype(F32).astype(BF16)
    gather_ref[...] = slot_rows(owned, pairs, gather_ref.shape[0] // owned)
    for copy in copies:
        copy.wait()


def harmonic_kernel(
    same, low_pairs, received_ref, weight_ref, sign_ref, gather_ref, hi_ref, lo_ref, out_ref, held
):
    owned, pair_total = hi_ref.shape[:2]
    low_total = lo_ref.shape[1]
    half = received_ref.shape[1] // HEMIS
    north = dot_tn(received_ref[:, :half], gather_ref[...])
    south = dot_tn(received_ref[:, half:], gather_ref[...])
    def analyse_slot(g):
        lanes = slice(g * pair_total, (g + 1) * pair_total)
        coeffs = jnp.concatenate([north[:, lanes], south[:, lanes]], axis=1).astype(BF16)
        hi_table = jnp.concatenate([hi_ref[g], hi_ref[g] * sign_ref[g]], axis=0)
        return (dot_nn(coeffs, hi_table) * weight_ref[g]).astype(BF16)

    alms = [analyse_slot(g) for g in range(1)]
    for g in range(owned):
        if g + 1 < owned:
            alms.append(analyse_slot(g + 1))
        lo_table = jnp.concatenate([lo_ref[g], lo_ref[g] * sign_ref[g]], axis=0)
        total = dot_nt(lo_table, alms[g]).astype(BF16)
        for h in range(HEMIS):
            held[g * low_total : (g + 1) * low_total, h * half : (h + 1) * half] = total[
                h * low_total : (h + 1) * low_total
            ]
    scatter = gather_ref[...] if same else slot_rows(owned, low_pairs, low_total)
    out_ref[...] = dot_nn(scatter, held[...]).astype(BF16)


def synthesise_kernel(
    phase_ref, table_ref, residue_ref, gather_ref, returned_ref, out_hbm,
    spectra, high, low, buffer, sems,
):
    pairs, steps, map_count, wide = buffer.shape[:4]
    count = phase_ref.shape[3]
    for j in range(count // LANES):
        rows = slice(j * LANES * pairs, (j + 1) * LANES * pairs)
        turned = dot_tn(returned_ref[rows], gather_ref[...])
        for p in range(pairs):
            spectra[p, :, j * LANES : (j + 1) * LANES] = turned[:, p * LANES : (p + 1) * LANES]

    south = (iota((F32_ROWS, count), 0) & 1) == 1

    def turn(p, i):
        def spread(c):
            north = spectra[p, c * map_count + i : c * map_count + i + 1]
            at = (2 + c) * map_count + i
            return jnp.where(south, spectra[p, at : at + 1], north)

        real, imag = spread(0), spread(1)
        cosine, sine = phase_ref[p, 0], phase_ref[p, 1]
        return real * cosine - imag * sine, imag * cosine + real * sine

    def rotate(p, first, last):
        for i in range(first, last, 2):
            at = slice((p * map_count + i) * F32_ROWS, (p * map_count + i + 2) * F32_ROWS)
            for c, parts in enumerate(zip(turn(p, i), turn(p, i + 1))):
                lanes = slice(c * count, (c + 1) * count)
                high[at, lanes], low[at, lanes] = split(jnp.concatenate(parts, axis=0))

    copies = []
    rotate(0, 0, map_count)
    for p in range(pairs):
        rows = slice(p * map_count * F32_ROWS, (p + 1) * map_count * F32_ROWS)
        for n in range(steps):
            lanes = slice(n * wide * LANES, (n + 1) * wide * LANES)
            pixels = dot_nn(high[rows], table_ref[:, lanes]) + dot_nn(low[rows], table_ref[:, lanes])
            pixels += dot_nn(high[rows], residue_ref[:, lanes])
            if p + 1 < pairs:
                share = map_count // steps
                rotate(p + 1, n * share, (n + 1) * share)
            pixels = pixels.reshape(map_count, F32_ROWS, wide * LANES)
            for a in range(wide):
                buffer[p, n, :, a] = pixels[:, :, a * LANES : (a + 1) * LANES]
            target = out_hbm.at[:, p, pl.ds(n * wide, wide)]
            copies.append(pltpu.make_async_copy(buffer.at[p, n], target, sems.at[p, n]))
            copies[-1].start()
    for copy in copies:
        copy.wait()


def vmem():
    return pl.BlockSpec(memory_space=pltpu.VMEM)


def smem():
    return pl.BlockSpec(memory_space=pltpu.SMEM)


def hbm():
    return pl.BlockSpec(memory_space=pltpu.HBM)


def params(grant=WHOLE_VMEM):
    return pltpu.CompilerParams(vmem_limit_bytes=grant)


def struct(shape, dtype):
    return jax.ShapeDtypeStruct(shape, dtype)


def analyse(sky_maps, hi_cycles, azimuth_orders):
    map_count, pairs = sky_maps.shape[:2]
    count = azimuth_orders.shape[0]
    cols = HEMIS * 2 * map_count
    inner = BF16_ROWS // HEMIS
    blocks = NPIX_HI // (inner * LANES)
    sky = sky_maps.reshape(map_count, pairs, HEMIS, blocks, inner, LANES)
    sky = sky.transpose(0, 1, 3, 4, 2, 5)
    sky = sky.reshape(map_count * pairs, blocks, BF16_ROWS, LANES)
    size = map_count // 4
    spans = []
    for k in range(4):
        edges = (0, blocks // 2, blocks) if k == 0 else (0, blocks)
        spans += [(k, k * size, size, *edge) for edge in zip(edges, edges[1:])]
    raw = pltpu.VMEM((size * pairs * BF16_ROWS, 2 * count), F32)
    return pl.pallas_call(
        functools.partial(analyse_kernel, spans),
        out_shape=struct((count * pairs, cols), BF16),
        in_specs=[hbm(), hbm(), hbm()],
        out_specs=vmem(),
        scratch_shapes=[
            pltpu.SMEM((pairs,), jnp.int32),
            pltpu.VMEM((1, count), jnp.int32),
            pltpu.VMEM((map_count * pairs, blocks, BF16_ROWS, LANES), BF16),
            pltpu.VMEM((blocks * LANES, 2 * count), BF16),
            raw,
            raw,
            pltpu.VMEM((pairs, HEMIS, 2, map_count, count), F32),
            pltpu.SemaphoreType.DMA((2 + len(spans),)),
        ],
        compiler_params=params(),
        name="analyse",
    )(hi_cycles, azimuth_orders.reshape(1, count), sky)


def per_device(
    sky_maps, hi_cycles, lo_cycles, azimuth_orders, legendre_hi, legendre_lo, beam_weights
):
    axes = ("band", "ma")
    map_count, pairs = sky_maps.shape[:2]
    low_pairs = lo_cycles.shape[0]
    count = azimuth_orders.shape[0]
    owned, degree_count, pair_total = legendre_hi.shape
    low_total = legendre_lo.shape[2]
    devices = count // owned
    order_row = azimuth_orders.reshape(1, count)
    order_column = azimuth_orders.reshape(count, 1)
    cols = HEMIS * 2 * map_count

    outgoing = analyse(sky_maps, hi_cycles, azimuth_orders)
    received = lax.all_to_all(
        outgoing.reshape(devices, owned * pairs, cols), axes, split_axis=0, concat_axis=0, tiled=True
    )

    rows = count * pairs
    own = lax.dynamic_slice_in_dim(azimuth_orders, lax.axis_index(axes) * owned, owned)
    low_rows = count * low_pairs
    same = (low_pairs, low_total) == (pairs, pair_total)
    hi_blocks, lo_blocks = legendre_hi.transpose(0, 2, 1), legendre_lo.transpose(0, 2, 1)
    prepared = pl.pallas_call(
        functools.partial(prepare_kernel, pairs),
        out_shape=[
            struct((owned, 1, degree_count), F32),
            struct((owned, 1, degree_count), BF16),
            struct((rows, owned * pair_total), BF16),
            struct(hi_blocks.shape, BF16),
            struct(lo_blocks.shape, BF16),
        ],
        in_specs=[smem(), vmem(), hbm(), hbm()],
        out_specs=[vmem()] * 5,
        scratch_shapes=[pltpu.SemaphoreType.DMA((2,))],
        compiler_params=params(50 * 2**20),
        cost_estimate=pl.CostEstimate(
            flops=2**10 * degree_count, bytes_accessed=2**10 * degree_count, transcendentals=0
        ),
        name="prepare",
    )(own, beam_weights.reshape(1, degree_count), hi_blocks, lo_blocks)
    synthesised = pl.pallas_call(
        functools.partial(harmonic_kernel, same, low_pairs),
        out_shape=struct((low_rows, cols), BF16),
        in_specs=[vmem()] * 6,
        out_specs=vmem(),
        scratch_shapes=[pltpu.VMEM((owned * low_total, cols), BF16)],
        compiler_params=params(16 * 2**20),
        name="harmonic",
    )(received.reshape(rows, cols), *prepared)
    returned = lax.all_to_all(
        synthesised.reshape(devices, owned * low_pairs, cols),
        axes,
        split_axis=0,
        concat_axis=0,
        tiled=True,
    )

    blocks_lo = NPIX_LO // (F32_ROWS // HEMIS * LANES)
    side = LANES * low_pairs
    inverse_table, residue, regroup, phase = pl.pallas_call(
        functools.partial(inverse_table_kernel, low_pairs),
        out_shape=[
            struct((2 * count, blocks_lo * LANES), BF16),
            struct((2 * count, blocks_lo * LANES), BF16),
            struct((side, side), BF16),
            struct((low_pairs, 2, F32_ROWS, count), F32),
        ],
        in_specs=[smem(), vmem(), vmem()],
        out_specs=[vmem()] * 4,
        compiler_params=params(8 * 2**20),
        cost_estimate=pl.CostEstimate(
            flops=64 * count * blocks_lo * LANES,
            bytes_accessed=8 * count * blocks_lo * LANES,
            transcendentals=0,
        ),
        name="inverse_table",
    )(lo_cycles, order_row, order_column)
    steps = 2
    wide = blocks_lo // steps
    buffer = pltpu.VMEM((low_pairs, steps, map_count, wide, F32_ROWS, LANES), F32)
    spectrum = pltpu.VMEM((map_count * low_pairs * F32_ROWS, 2 * count), BF16)
    pixels = pl.pallas_call(
        synthesise_kernel,
        out_shape=struct((map_count, low_pairs, blocks_lo, F32_ROWS, LANES), F32),
        in_specs=[vmem()] * 5,
        out_specs=hbm(),
        scratch_shapes=[
            pltpu.VMEM((low_pairs, cols, count), F32),
            spectrum,
            spectrum,
            buffer,
            pltpu.SemaphoreType.DMA((low_pairs, steps)),
        ],
        compiler_params=params(32 * 2**20),
        name="synthesise",
    )(phase, inverse_table, residue, regroup, returned.reshape(low_rows, cols))
    pixels = pixels.reshape(map_count, low_pairs, blocks_lo, F32_ROWS // HEMIS, HEMIS, LANES)
    pixels = pixels.transpose(0, 1, 4, 2, 3, 5)
    return pixels.reshape(map_count, low_pairs, HEMIS, NPIX_LO)


def solution(mesh):
    spread = ("band", "ma")
    return jax.shard_map(
        per_device,
        mesh=mesh,
        in_specs=(
            P(None, spread, None, None),
            P(spread),
            P(spread),
            P(),
            P(spread, None, None),
            P(spread, None, None),
            P(),
        ),
        out_specs=P(None, spread, None, None),
        check_vma=False,
    )
```
